32 devices in a mesh: grp: 2 (over x), lat: 16 (over z, y, core).
Axes of the slice: x: 2, y: 2, z: 4, core: 2. Of those that a mesh axis runs over, the one named last changes fastest.
Arguments:
- coarse: bfloat16 [80, 64, 512], P(None, ('grp', 'lat')), parts along dimension 1, may hold values from -6 to 6
- reg_gain: float32 [2, 80], replicated, may hold values from 0.25 to 1.75
- reg_weight: bfloat16 [2, 3, 3, 80, 80], replicated, may hold values from -0.21875 to 0.21875
- reg_bias: float32 [2, 80], replicated, may hold values from -1.5 to 1.5
- noisy: bfloat16 [32, 4, 32, 512], P(('grp', 'lat')), parts along dimension 0, may hold values from -6 to 6
- lift_weight: bfloat16 [3, 3, 192, 84], replicated, may hold values from -0.21875 to 0.21875
- lift_bias: float32 [192], replicated, may hold values from -1.5 to 1.5
- mid_gain: float32 [192], replicated, may hold values from 0.25 to 1.75
- mid_weight: bfloat16 [3, 3, 192, 192], replicated, may hold values from -0.15625 to 0.15625
- mid_bias: float32 [192], replicated, may hold values from -1.5 to 1.5
Outputs:
- fine_level: bfloat16 [32, 192, 32, 512], P(('grp', 'lat')), parts along dimension 0
The draws below stay inside these ranges and needn't reach their ends.
There are 2 independent parts, one for each index of `grp`. The reference program is written for one: setup_inputs(seed, part) draws one part's arguments, and reference() takes and returns one part's arrays. A program takes and returns all parts, laid end to end along the dimension named above; an argument that names none is the same for every part. Nothing has to cross between parts.
All inputs are finite; a program needn't handle non-finite values.
Results may differ from the reference program's by a relative error of at most 0.007.
Values may be sent and summed in bfloat16 or wider, within the bound.
A program may use at most 320 MiB of HBM per device.

```python
import jax
import jax.numpy as jnp
from jax import lax

CIN = 80
CH = 192
NOUT = 4
REG_BLOCKS = 2
CLON = 512
TILE_COLS = 4
LAT_UP = 4
LON_UP = 4
NCR = 32
TILE_ROWS = 4
FT_ROWS = 32
FT_LON = 512
FLAT = 128
FLON = 2048
N_LAT = 16


def shard_levels(own_key, extent, cuts, least, top_value):
    def one(dim, blocks):
        draws = jax.random.uniform(jax.random.fold_in(jax.random.fold_in(own_key, 6), dim), (blocks,), jnp.float32, least / len(cuts), top_value / len(cuts))
        return jnp.repeat(jnp.exp(draws), extent[dim] // blocks).reshape((-1,) + (1,) * (len(extent) - dim - 1))

    level = one(*cuts[0])
    for cut in cuts[1:]:
        level = level * one(*cut)
    return level


def gaussian(key, shape, width, bound, shards=(), kind=jnp.bfloat16):
    level = shard_levels(key, shape, shards, -0.22, 0.18) if shards else 1.0
    entries = jax.random.normal(key, shape, jnp.float32) * width * level
    return jnp.minimum(jnp.maximum(entries, -bound), bound).astype(kind)


def setup_inputs(seed: int = 0, part: int = 0) -> dict:
    arg_keys = jax.random.split(jax.random.key(seed), 11)
    part_splits = jax.random.split(jax.random.fold_in(arg_keys[10], part), 11)
    coarse = gaussian(part_splits[0], (CIN, NCR, CLON), 1.0, 6.0, ((1, 16),))
    reg_gain = jnp.clip(1.0 + 0.15 * jax.random.normal(arg_keys[1], (REG_BLOCKS, CIN), jnp.float32), 0.25, 1.75)
    reg_weight = gaussian(arg_keys[2], (REG_BLOCKS, 3, 3, CIN, CIN), (9 * CIN) ** -0.5, 0.21875)
    reg_bias = gaussian(arg_keys[3], (REG_BLOCKS, CIN), 0.3, 1.5, (), jnp.float32)
    noisy = gaussian(part_splits[4], (N_LAT, NOUT, FT_ROWS, FT_LON), 1.0, 6.0, ((0, 16),))
    lift_weight = gaussian(arg_keys[5], (3, 3, CH, CIN + NOUT), (9 * (CIN + NOUT)) ** -0.5, 0.21875)
    lift_bias = gaussian(arg_keys[6], (CH,), 0.3, 1.5, (), jnp.float32)
    mid_gain = jnp.clip(1.0 + 0.15 * jax.random.normal(arg_keys[7], (CH,), jnp.float32), 0.25, 1.75)
    mid_weight = gaussian(arg_keys[8], (3, 3, CH, CH), (9 * CH) ** -0.5, 0.15625)
    mid_bias = gaussian(arg_keys[9], (CH,), 0.3, 1.5, (), jnp.float32)
    return dict(coarse=coarse, reg_gain=reg_gain, reg_weight=reg_weight, reg_bias=reg_bias, noisy=noisy, lift_weight=lift_weight, lift_bias=lift_bias, mid_gain=mid_gain, mid_weight=mid_weight, mid_bias=mid_bias)


EPSILON = 1e-06
HIGHEST = lax.Precision.HIGHEST

def activate(field_in, gain_row):
    values = field_in.astype(jnp.float32)
    inverse = lax.rsqrt(lax.optimization_barrier(jnp.mean(values * values, axis=0, keepdims=True)) + EPSILON)
    return jax.nn.silu(values * inverse * gain_row[:, None, None]).astype(jnp.bfloat16)

def wrap_cols(field_in):
    return jnp.concatenate([field_in[:, :, -1:], field_in, field_in[:, :, :1]], axis=2)

def pad_rows(field_in):
    return jnp.pad(field_in, ((0, 0), (1, 1), (0, 0)))

def conv_taps(padded, weight):
    channels = padded.shape[0]
    height = padded.shape[1] - 2
    breadth = padded.shape[2] - 2
    summed = jnp.zeros((weight.shape[2], height * breadth), jnp.float32)
    for row_shift in range(3):
        for col_shift in range(3):
            window = padded[:, row_shift:row_shift + height, col_shift:col_shift + breadth].reshape(channels, height * breadth)
            summed = summed + jnp.dot(weight[row_shift, col_shift], window, preferred_element_type=jnp.float32)
    return summed.reshape(weight.shape[2], height, breadth)

def blend_matrix(fine_count, coarse_count, factor, clamped):
    fine_index = jnp.arange(fine_count, dtype=jnp.int32)
    numerator = 2 * fine_index + 1 - factor
    lower_cell = numerator // (2 * factor)
    fraction = (numerator - 2 * factor * lower_cell).astype(jnp.float32) / (2.0 * factor)
    if clamped:
        low_side = numerator < 0
        high_side = lower_cell >= coarse_count - 1
        lower_cell = jnp.where(low_side, 0, jnp.where(high_side, coarse_count - 1, lower_cell))
        fraction = jnp.where(low_side | high_side, 0.0, fraction)
        upper_cell = lower_cell + 1
    else:
        lower_cell = lower_cell % coarse_count
        upper_cell = (lower_cell + 1) % coarse_count
    columns = jnp.arange(coarse_count, dtype=jnp.int32)[None, :]
    first_part = jnp.where(columns == lower_cell[:, None], 1.0 - fraction[:, None], 0.0)
    second_part = jnp.where(columns == upper_cell[:, None], fraction[:, None], 0.0)
    return (first_part + second_part).astype(jnp.float32)

def reference(coarse, reg_gain, reg_weight, reg_bias, noisy, lift_weight, lift_bias, mid_gain, mid_weight, mid_bias):
    current = coarse
    for block_index in range(REG_BLOCKS):
        activated = activate(current, reg_gain[block_index])
        update = conv_taps(wrap_cols(pad_rows(activated)), reg_weight[block_index])
        updated = current.astype(jnp.float32) + update + reg_bias[block_index][:, None, None]
        current = lax.optimization_barrier(updated.astype(jnp.bfloat16))
    lat_blend = blend_matrix(FLAT, NCR, LAT_UP, True)
    lon_blend = blend_matrix(FLON, CLON, LON_UP, False)
    halfway = jnp.einsum('yi,cij->cyj', lat_blend, current.astype(jnp.float32), precision=HIGHEST)
    upsampled = jnp.einsum('cyj,xj->cyx', halfway, lon_blend, precision=HIGHEST).astype(jnp.bfloat16)
    noise_field = noisy.reshape(TILE_ROWS, TILE_COLS, NOUT, FT_ROWS, FT_LON).transpose(2, 0, 3, 1, 4).reshape(NOUT, FLAT, FLON)
    lift_input = jnp.concatenate([upsampled, noise_field], axis=0)
    lifted = conv_taps(wrap_cols(pad_rows(lift_input)), lift_weight) + lift_bias[:, None, None]
    lifted = lax.optimization_barrier(lifted.astype(jnp.bfloat16))
    activated = activate(lifted, mid_gain)
    summed = lifted.astype(jnp.float32) + conv_taps(wrap_cols(pad_rows(activated)), mid_weight) + mid_bias[:, None, None]
    fine_level = summed.astype(jnp.bfloat16)
    return fine_level.reshape(CH, TILE_ROWS, FT_ROWS, TILE_COLS, FT_LON).transpose(1, 3, 0, 2, 4).reshape(N_LAT, CH, FT_ROWS, FT_LON)
```

```python
import functools

import jax
import jax.numpy as jnp
from jax import lax
from jax.experimental import pallas as pl
from jax.experimental.pallas import tpu as pltpu
from jax.sharding import PartitionSpec as P

TILE_COLS = 4
LAT_UP = 4
LON_UP = 4
EPSILON = 1e-06
F32 = jnp.float32
BF16 = jnp.bfloat16
MESH = pl.DeviceIdType.MESH
HALF = 64


def gather_kernel(pieces, cols, rows, got, got_cols, got_rows, send, recv, nsend, nrecv, local):
    me = lax.axis_index("lat")
    tile_rows = lax.axis_size("lat") // TILE_COLS
    r = me // TILE_COLS
    c = me % TILE_COLS
    north, south = r > 0, r < tile_rows - 1

    barrier = pltpu.get_barrier_semaphore()

    def greet(target):
        pl.semaphore_signal(barrier, inc=1, device_id={"lat": target}, device_id_type=MESH)

    for k in range(1, TILE_COLS):
        greet(r * TILE_COLS + (c + k) % TILE_COLS)

    @pl.when(north)
    def _():
        for k in range(TILE_COLS):
            greet((r - 1) * TILE_COLS + k)

    @pl.when(south)
    def _():
        for k in range(TILE_COLS):
            greet((r + 1) * TILE_COLS + k)

    peers = TILE_COLS - 1 + jnp.where(north, TILE_COLS, 0) + jnp.where(south, TILE_COLS, 0)
    pl.semaphore_wait(barrier, peers)

    def remote(src, dst, ssem, rsem, target):
        return pltpu.make_async_remote_copy(
            src_ref=src, dst_ref=dst, send_sem=ssem, recv_sem=rsem,
            device_id={"lat": target}, device_id_type=MESH)

    def band_copy(k, row, slot, ssem):
        col = (c + k) % TILE_COLS
        return remote(pieces.at[col], got.at[slot], send.at[ssem], recv.at[slot], row * TILE_COLS + col)

    west, east = (c + TILE_COLS - 1) % TILE_COLS, (c + 1) % TILE_COLS

    def col_copy(slot, row, col):
        return remote(cols, got_cols.at[slot], nsend.at[slot], nrecv.at[slot], row * TILE_COLS + col)

    def row_copy(slot, row):
        return remote(rows, got_rows.at[slot], nsend.at[6 + slot], nrecv.at[6 + slot], row * TILE_COLS + c)

    low, high = c < 2, c >= 2

    def each(action):
        @pl.when(jnp.logical_and(south, high))
        def _():
            for k in range(TILE_COLS):
                action(band_copy(k, r + 1, c - 2, TILE_COLS + k))

        @pl.when(jnp.logical_and(north, low))
        def _():
            for k in range(TILE_COLS):
                action(band_copy(k, r - 1, 6 + c, TILE_COLS + k))

        for k in range(1, TILE_COLS):
            action(band_copy(k, r, 2 + c, k))
        action(col_copy(0, r, east))
        action(col_copy(1, r, west))

        @pl.when(south)
        def _():
            action(row_copy(0, r + 1))
            action(col_copy(2, r + 1, east))
            action(col_copy(3, r + 1, west))

        @pl.when(north)
        def _():
            action(row_copy(1, r - 1))
            action(col_copy(4, r - 1, east))
            action(col_copy(5, r - 1, west))

    each(lambda copy: copy.start())
    own = pltpu.make_async_copy(pieces.at[c], got.at[2 + c], local)
    own.start()
    own.wait()
    each(lambda copy: copy.wait_send())

    def arrived(slot):
        remote(pieces.at[0], got.at[slot], send.at[0], recv.at[slot], me).wait_recv()

    def edge(slot):
        if slot < 6:
            remote(cols, got_cols.at[slot], nsend.at[slot], nrecv.at[slot], me).wait_recv()
        else:
            remote(rows, got_rows.at[slot - 6], nsend.at[slot], nrecv.at[slot], me).wait_recv()

    for k in range(1, TILE_COLS):
        arrived(2 + (c + k) % TILE_COLS)
    edge(0)
    edge(1)

    @pl.when(north)
    def _():
        arrived(0)
        arrived(1)
        edge(2)
        edge(3)
        edge(6)

    @pl.when(south)
    def _():
        arrived(6)
        arrived(7)
        edge(4)
        edge(5)
        edge(7)


def gather(pieces, cols, rows):
    any_space = pl.BlockSpec(memory_space=pl.ANY)
    dma = pltpu.SemaphoreType.DMA
    return pl.pallas_call(
        gather_kernel,
        out_shape=(
            jax.ShapeDtypeStruct((8,) + pieces.shape[1:], BF16),
            jax.ShapeDtypeStruct((6,) + cols.shape, BF16),
            jax.ShapeDtypeStruct((2,) + rows.shape, BF16),
        ),
        in_specs=[any_space] * 3,
        out_specs=(any_space,) * 3,
        scratch_shapes=[dma((2 * TILE_COLS,)), dma((8,)), dma((8,)), dma((8,)), dma],
        compiler_params=pltpu.CompilerParams(collective_id=0, has_side_effects=True),
    )(pieces, cols, rows)


def silu(values):
    return 0.5 * values * (1.0 + jnp.tanh(0.5 * values))


def activate(values, gain):
    inverse = lax.rsqrt(jnp.mean(values * values, axis=0, keepdims=True) + EPSILON)
    return silu(values * inverse * gain)


def split(numerator, factor):
    lower = numerator // (2 * factor)
    return lower, (numerator - 2 * factor * lower).astype(F32) / (2.0 * factor)


def tile_kernel(
    dims, info, got, gain, regw, regb, noise, noise_edge, liftw, liftb, midg, midw, midb, out,
    taps, field, lon, lines, upper, sides, bands, keep, rows_out, stage, sems,
):
    cin, ch, ct, fr, fl = dims
    bands_n = got.shape[0]
    cw = got.shape[2]
    ccols = fl // LON_UP
    tile_row, tile_rows = info[0], info[1]
    top, bottom = tile_row == 0, tile_row == tile_rows - 1
    spare = (bands_n - ct) // 2

    def real(i):
        row = tile_row * ct - spare + i
        return jnp.logical_and(row >= 0, row < ct * tile_rows)

    blocks = regw.shape[0]
    for k in range(blocks):
        first, last = 1 + k, bands_n - 1 - k

        def fill(i, _, k=k):
            source = got[i] if k == 0 else field[i]
            values = jnp.where(real(i), source.astype(F32), 0.0)
            values = jnp.where(real(i), activate(values, gain[k]), 0.0)
            base = pl.multiple_of(i * 3 * cin, 16)
            taps[pl.ds(base, cin), :] = pltpu.roll(values, 1, 1).astype(BF16)
            taps[pl.ds(base + cin, cin), :] = values.astype(BF16)
            taps[pl.ds(base + 2 * cin, cin), :] = pltpu.roll(values, cw - 1, 1).astype(BF16)
            return 0

        lax.fori_loop(first, last, fill, 0)

        def conv(i, _, k=k):
            base = pl.multiple_of((i - 1) * 3 * cin, 16)
            update = jnp.dot(regw[k], taps[pl.ds(base, 9 * cin), :], preferred_element_type=F32)
            source = got[i] if k == 0 else field[i]
            field[i] = jnp.where(real(i), source.astype(F32) + update + regb[k], 0.0).astype(BF16)
            return 0

        lax.fori_loop(first + 1, last - 1, conv, 0)

    first = 1 + blocks
    count = bands_n - 2 * first
    coarse_lane = lax.broadcasted_iota(jnp.int32, (cw, 3 * fl), 0)
    position = lax.broadcasted_iota(jnp.int32, (cw, 3 * fl), 1)

    def lon_weights(fine_col, lane):
        lower, part = split(2 * fine_col + 1 - LON_UP, LON_UP)
        low_lane = jnp.where(lower < 0, lower + cw, lower)
        high_lane = jnp.where(lower + 1 < 0, lower + 1 + cw, lower + 1)
        return (jnp.where(lane == low_lane, 1.0 - part, 0.0)
                + jnp.where(lane == high_lane, part, 0.0)).astype(BF16)

    shift = jnp.where(position >= 2 * fl, 2, jnp.where(position >= fl, 1, 0))
    lon[...] = lon_weights(position - shift * fl + shift - 1, coarse_lane)
    edge_lane = lax.broadcasted_iota(jnp.int32, (cw, 128), 0)
    edge_pos = lax.broadcasted_iota(jnp.int32, (cw, 128), 1)
    edge_col = jnp.where(edge_pos < 3, edge_pos - 2, fl - 4 + edge_pos)
    edge_weights = lon_weights(edge_col, edge_lane)

    def widen(i, _):
        for q in range(3):
            lines[i, q * cin:(q + 1) * cin, :] = jnp.dot(
                field[i + first], lon[:, q * fl:(q + 1) * fl], preferred_element_type=F32)
        return 0

    lax.fori_loop(0, count, widen, 0)

    low_line = jnp.where(top, 1, 0)
    high_line = jnp.where(bottom, count - 2, count - 1)
    fine_total = fr * tile_rows

    def inside(t):
        row = tile_row * fr + t - 2
        return jnp.logical_and(row >= 0, row < fine_total)

    slab = 3 * cin + noise.shape[1]

    def raise_row(t):
        lower, part = split(2 * (t - 2) + 1 - LAT_UP + 2 * LAT_UP, LAT_UP)
        a = jnp.clip(lower, low_line, high_line)
        b = jnp.clip(lower + 1, low_line, high_line)
        blended = (1.0 - part) * lines[a] + part * lines[b]
        base = pl.multiple_of(t * slab, 16)
        upper[pl.ds(base, 3 * cin), :] = jnp.where(inside(t), blended, 0.0).astype(BF16)
        upper[pl.ds(base + 3 * cin, noise.shape[1]), :] = noise[t]

    lane = lax.broadcasted_iota(jnp.int32, (1, 128), 1)
    left = lane < HALF
    edge_row = jnp.where(left, lane, lane - HALF)
    sums = [[jnp.zeros((cin, 128), F32) for _ in range(3)] for _ in range(3)]
    weights = []
    for p in range(3):
        t = edge_row + p
        lower, part = split(2 * (t - 2) + 1 - LAT_UP + 2 * LAT_UP, LAT_UP)
        a = jnp.clip(lower, low_line, high_line)
        b = jnp.clip(lower + 1, low_line, high_line)
        ok = inside(t)
        weights.append([jnp.where(ok, jnp.where(a == i, 1.0 - part, 0.0) + jnp.where(b == i, part, 0.0), 0.0)
                        for i in range(count)])
    for i in range(count):
        narrow = jnp.dot(field[first + i], edge_weights, preferred_element_type=F32)
        for q in range(3):
            column = jnp.where(left, narrow[:, q:q + 1], narrow[:, 3 + q:4 + q])
            for p in range(3):
                sums[p][q] = sums[p][q] + weights[p][i] * column
    for p in range(3):
        for q in range(3):
            base = p * slab + q * cin
            sides[base:base + cin, :] = sums[p][q].astype(BF16)
        sides[p * slab + 3 * cin:(p + 1) * slab, :] = noise_edge[p]
    edge_lift = jnp.dot(liftw[...], sides[...], preferred_element_type=F32) + liftb[...]
    edge_lift = edge_lift.astype(BF16).astype(F32)
    edge_act = jnp.where(inside(edge_row + 1), activate(edge_lift, midg[...]), 0.0)

    for t in range(3):
        raise_row(jnp.int32(t))

    lane_full = lax.broadcasted_iota(jnp.int32, (1, fl), 1)
    kept = keep.shape[0]
    group = stage.shape[2]

    def lift(l):
        base = pl.multiple_of(l * slab, 16)
        return jnp.dot(liftw[...], upper[pl.ds(base, 3 * slab), :], preferred_element_type=F32) + liftb[...]

    def finish(l, lifted):
        rounded = lifted.astype(BF16)
        keep[l % kept] = rounded
        values = jnp.where(inside(l + 1), activate(rounded.astype(F32), midg[...]), 0.0)
        turned = pltpu.roll(edge_act, 128 - l, 1)
        edge_l = jnp.concatenate([turned[:, :128]] + [turned] * (fl // 128 - 1), axis=1)
        turned_r = pltpu.roll(edge_act, HALF - 1 - l + 128, 1)
        edge_r = jnp.concatenate([turned_r] * (fl // 128), axis=1)
        base = pl.multiple_of(l * 3 * ch, 16)
        bands[pl.ds(base, ch), :] = jnp.where(lane_full == 0, edge_l, pltpu.roll(values, 1, 1)).astype(BF16)
        bands[pl.ds(base + ch, ch), :] = values.astype(BF16)
        bands[pl.ds(base + 2 * ch, ch), :] = jnp.where(
            lane_full == fl - 1, edge_r, pltpu.roll(values, fl - 1, 1)).astype(BF16)

    def mid(y):
        base = pl.multiple_of(y * 3 * ch, 16)
        return jnp.dot(midw[...], bands[pl.ds(base, 9 * ch), :], preferred_element_type=F32)

    def flush(y):
        part = y // group
        slot = part % 2

        def copy(n):
            return pltpu.make_async_copy(
                stage.at[n % 2], out.at[0, :, pl.ds(pl.multiple_of(n * group, group), group), :], sems.at[n % 2])

        @pl.when(part >= 2)
        def _():
            copy(part - 2).wait()

        def shrink(o, _):
            for j in range(fl // 128):
                block = rows_out[j, pl.ds(pl.multiple_of(o * 8 * group, 8 * group), 8 * group), :]
                stage[slot, pl.ds(o * 8, 8), :, j * 128:(j + 1) * 128] = block.reshape(8, group, 128).astype(BF16)
            return 0

        lax.fori_loop(0, ch // 8, shrink, 0)
        copy(part).start()

    def emit(y, product):
        total = keep[(y + 1) % kept].astype(F32) + product + midb[...]
        for j in range(fl // 128):
            rows_out[j, pl.ds(y % group, ch, stride=group), :] = total[:, j * 128:(j + 1) * 128]

        @pl.when(y % group == group - 1)
        def _():
            flush(y)

    def lead(l, _):
        lifted = lift(l)
        raise_row(l + 3)
        finish(l, lifted)
        return 0

    lax.fori_loop(0, 3, lead, 0)

    def both(l, _):
        lifted = lift(l)
        product = mid(l - 3)
        raise_row(jnp.minimum(l + 3, fr + 3))
        finish(l, lifted)
        emit(l - 3, product)
        return 0

    lax.fori_loop(3, fr + 2, both, 0)
    emit(fr - 1, mid(fr - 1))
    parts = fr // group
    for n in range(max(parts - 2, 0), parts):
        pltpu.make_async_copy(stage.at[n % 2], out.at[0, :, pl.ds(n * group, group), :], sems.at[n % 2]).wait()


def tile_program(info, got, gain, regw, regb, noise, noise_edge, liftw, liftb, midg, midw, midb, ct):
    cin, cw = got.shape[1], got.shape[2]
    ch = liftw.shape[0]
    fr, fl = noise.shape[0] - 4, noise.shape[2]
    count = ct + 2
    group = 16
    vmem = pl.BlockSpec(memory_space=pltpu.VMEM)
    slab = 3 * cin + noise.shape[1]
    return pl.pallas_call(
        functools.partial(tile_kernel, (cin, ch, ct, fr, fl)),
        out_shape=jax.ShapeDtypeStruct((1, ch, fr, fl), BF16),
        in_specs=[pl.BlockSpec(memory_space=pltpu.SMEM)] + [vmem] * 11,
        out_specs=pl.BlockSpec(memory_space=pl.ANY),
        scratch_shapes=[
            pltpu.VMEM((got.shape[0] * 3 * cin, cw), BF16),
            pltpu.VMEM(got.shape, BF16),
            pltpu.VMEM((cw, 3 * fl), BF16),
            pltpu.VMEM((count, 3 * cin, fl), F32),
            pltpu.VMEM(((fr + 4) * slab, fl), BF16),
            pltpu.VMEM((3 * slab, 128), BF16),
            pltpu.VMEM(((fr + 2) * 3 * ch, fl), BF16),
            pltpu.VMEM((8, ch, fl), BF16),
            pltpu.VMEM((fl // 128, ch * group, 128), F32),
            pltpu.VMEM((2, ch, group, fl), BF16),
            pltpu.SemaphoreType.DMA((2,)),
        ],
        compiler_params=pltpu.CompilerParams(vmem_limit_bytes=66_000_000),
    )(info, got, gain, regw, regb, noise, noise_edge, liftw, liftb, midg, midw, midb)


def per_device(
    coarse, reg_gain, reg_weight, reg_bias, noisy, lift_weight, lift_bias, mid_gain, mid_weight, mid_bias,
):
    device = lax.axis_index("lat")
    tile_rows = lax.axis_size("lat") // TILE_COLS
    cin, band_rows, clon = coarse.shape
    ct = band_rows * TILE_COLS
    ct_lon = clon // TILE_COLS
    blocks = reg_weight.shape[0]
    ch = lift_weight.shape[2]
    nout = noisy.shape[1]
    fr, fl = noisy.shape[2], noisy.shape[3]

    wide = coarse.reshape(cin, band_rows, TILE_COLS, ct_lon)
    after = jnp.roll(wide, -1, axis=2)
    before = jnp.roll(wide, 1, axis=2)
    side = jnp.where(jnp.arange(ct_lon) < ct_lon // 2, after, before)
    pieces = jnp.concatenate([wide, side], axis=3).transpose(2, 1, 0, 3)

    tile = noisy[0]
    edge_cols = jnp.concatenate([tile[:, :, :2], tile[:, :, -2:]], axis=2).transpose(0, 2, 1)
    edge_cols = jnp.pad(edge_cols.reshape(nout * 4, fr), ((0, 0), (0, 128 - fr)))
    edge_rows = jnp.concatenate([tile[:, :2], tile[:, -2:]], axis=1).reshape(nout * 4, fl)

    got, got_cols, got_rows = gather(pieces, edge_cols, edge_rows)

    tile_row = device // TILE_COLS
    has_north = tile_row > 0
    has_south = tile_row < tile_rows - 1
    nc = got_cols[:, :, :fr].reshape(6, nout, 4, fr).transpose(0, 1, 3, 2)
    nr = got_rows.reshape(2, nout, 4, fl)
    zero = jnp.zeros((), BF16)
    north = jnp.where(has_north, jnp.concatenate([nc[2][:, -2:, 2:], nr[0][:, 2:], nc[3][:, -2:, :2]], axis=2), zero)
    south = jnp.where(has_south, jnp.concatenate([nc[4][:, :2, 2:], nr[1][:, :2], nc[5][:, :2, :2]], axis=2), zero)
    middle = jnp.concatenate([nc[0][:, :, 2:], tile, nc[1][:, :, :2]], axis=2)
    whole = jnp.concatenate([north, middle, south], axis=1).transpose(1, 0, 2)
    spare = (-3 * nout) % 16
    noise = jnp.concatenate(
        [whole[:, :, 1 + q:1 + q + fl] for q in range(3)] + [jnp.zeros((fr + 4, spare, fl), BF16)], axis=1)
    sides = []
    for p in range(3):
        per_shift = []
        for q in range(3):
            lo = jnp.pad(whole[p:p + fr + 2, :, q].T, ((0, 0), (0, HALF - fr - 2)))
            hi = jnp.pad(whole[p:p + fr + 2, :, fl + 1 + q].T, ((0, 0), (0, HALF - fr - 2)))
            per_shift.append(jnp.concatenate([lo, hi], axis=1))
        sides.append(jnp.concatenate(per_shift + [jnp.zeros((spare, 128), BF16)], axis=0))
    noise_edge = jnp.stack(sides)

    regw = reg_weight.transpose(0, 3, 1, 2, 4).reshape(blocks, cin, 9 * cin)
    up = lift_weight[..., :cin].transpose(2, 0, 1, 3).reshape(ch, 3, 3 * cin)
    down = lift_weight[..., cin:].transpose(2, 0, 1, 3).reshape(ch, 3, 3 * nout)
    liftw = jnp.concatenate([up, down, jnp.zeros((ch, 3, spare), BF16)], axis=2).reshape(ch, -1)
    midw = mid_weight.transpose(2, 0, 1, 3).reshape(ch, 9 * ch)
    info = jnp.stack([tile_row, jnp.int32(tile_rows)]).astype(jnp.int32)
    got = got.reshape((got.shape[0] * band_rows,) + got.shape[2:])
    return tile_program(
        info, got, reg_gain[:, :, None], regw, reg_bias[:, :, None], noise, noise_edge,
        liftw, lift_bias[:, None], mid_gain[:, None], midw, mid_bias[:, None], ct)


def solution(mesh):
    placed = (
        P(None, ("grp", "lat"), None),
        P(),
        P(),
        P(),
        P(("grp", "lat"), None, None, None),
        P(),
        P(),
        P(),
        P(),
        P(),
    )
    return jax.shard_map(
        per_device,
        mesh=mesh,
        in_specs=placed,
        out_specs=P(("grp", "lat"), None, None, None),
        check_vma=False,
    )
```

```python
import functools

import jax
import jax.numpy as jnp
from jax import lax
from jax.experimental import pallas as pl
from jax.experimental.pallas import tpu as pltpu
from jax.sharding import PartitionSpec as P

TILE_COLS = 4
LAT_UP = 4
LON_UP = 4
EPSILON = 1e-06
F32 = jnp.float32
BF16 = jnp.bfloat16
MESH = pl.DeviceIdType.MESH
HALF = 64


def gather_kernel(pieces, cols, rows, got, got_cols, got_rows, send, recv, nsend, nrecv, local):
    me = lax.axis_index("lat")
    tile_rows = lax.axis_size("lat") // TILE_COLS
    r = me // TILE_COLS
    c = me % TILE_COLS
    north, south = r > 0, r < tile_rows - 1

    barrier = pltpu.get_barrier_semaphore()

    def greet(target):
        pl.semaphore_signal(barrier, inc=1, device_id={"lat": target}, device_id_type=MESH)

    for k in range(1, TILE_COLS):
        greet(r * TILE_COLS + (c + k) % TILE_COLS)

    @pl.when(north)
    def _():
        for k in range(TILE_COLS):
            greet((r - 1) * TILE_COLS + k)

    @pl.when(south)
    def _():
        for k in range(TILE_COLS):
            greet((r + 1) * TILE_COLS + k)

    peers = TILE_COLS - 1 + jnp.where(north, TILE_COLS, 0) + jnp.where(south, TILE_COLS, 0)
    pl.semaphore_wait(barrier, peers)

    def remote(src, dst, ssem, rsem, target):
        return pltpu.make_async_remote_copy(
            src_ref=src, dst_ref=dst, send_sem=ssem, recv_sem=rsem,
            device_id={"lat": target}, device_id_type=MESH)

    def band_copy(k, row, slot, ssem):
        col = (c + k) % TILE_COLS
        return remote(pieces.at[col], got.at[slot], send.at[ssem], recv.at[slot], row * TILE_COLS + col)

    west, east = (c + TILE_COLS - 1) % TILE_COLS, (c + 1) % TILE_COLS

    def col_copy(slot, row, col):
        return remote(cols, got_cols.at[slot], nsend.at[slot], nrecv.at[slot], row * TILE_COLS + col)

    def row_copy(slot, row):
        return remote(rows, got_rows.at[slot], nsend.at[6 + slot], nrecv.at[6 + slot], row * TILE_COLS + c)

    low, high = c < 2, c >= 2

    def each(action):
        @pl.when(jnp.logical_and(south, high))
        def _():
            for k in range(TILE_COLS):
                action(band_copy(k, r + 1, c - 2, TILE_COLS + k))

        @pl.when(jnp.logical_and(north, low))
        def _():
            for k in range(TILE_COLS):
                action(band_copy(k, r - 1, 6 + c, TILE_COLS + k))

        for k in range(1, TILE_COLS):
            action(band_copy(k, r, 2 + c, k))
        action(col_copy(0, r, east))
        action(col_copy(1, r, west))

        @pl.when(south)
        def _():
            action(row_copy(0, r + 1))
            action(col_copy(2, r + 1, east))
            action(col_copy(3, r + 1, west))

        @pl.when(north)
        def _():
            action(row_copy(1, r - 1))
            action(col_copy(4, r - 1, east))
            action(col_copy(5, r - 1, west))

    each(lambda copy: copy.start())
    own = pltpu.make_async_copy(pieces.at[c], got.at[2 + c], local)
    own.start()
    own.wait()
    each(lambda copy: copy.wait_send())

    def arrived(slot):
        remote(pieces.at[0], got.at[slot], send.at[0], recv.at[slot], me).wait_recv()

    def edge(slot):
        if slot < 6:
            remote(cols, got_cols.at[slot], nsend.at[slot], nrecv.at[slot], me).wait_recv()
        else:
            remote(rows, got_rows.at[slot - 6], nsend.at[slot], nrecv.at[slot], me).wait_recv()

    for k in range(1, TILE_COLS):
        arrived(2 + (c + k) % TILE_COLS)
    edge(0)
    edge(1)

    @pl.when(north)
    def _():
        arrived(0)
        arrived(1)
        edge(2)
        edge(3)
        edge(6)

    @pl.when(south)
    def _():
        arrived(6)
        arrived(7)
        edge(4)
        edge(5)
        edge(7)


def gather(pieces, cols, rows):
    any_space = pl.BlockSpec(memory_space=pl.ANY)
    dma = pltpu.SemaphoreType.DMA
    return pl.pallas_call(
        gather_kernel,
        out_shape=(
            jax.ShapeDtypeStruct((8,) + pieces.shape[1:], BF16),
            jax.ShapeDtypeStruct((6,) + cols.shape, BF16),
            jax.ShapeDtypeStruct((2,) + rows.shape, BF16),
        ),
        in_specs=[any_space] * 3,
        out_specs=(any_space,) * 3,
        scratch_shapes=[dma((2 * TILE_COLS,)), dma((8,)), dma((8,)), dma((8,)), dma],
        compiler_params=pltpu.CompilerParams(collective_id=0, has_side_effects=True),
    )(pieces, cols, rows)


def activate(values, half_gain):
    inverse = lax.rsqrt(jnp.mean(values * values, axis=0, keepdims=True) + EPSILON)
    half = values * inverse * half_gain
    return half + half * jnp.tanh(half)


def split(numerator, factor):
    lower = numerator // (2 * factor)
    return lower, (numerator - 2 * factor * lower).astype(F32) / (2.0 * factor)


def column(row):
    n = row.shape[1]
    here = lax.broadcasted_iota(jnp.int32, (n, n), 0) == lax.broadcasted_iota(jnp.int32, (n, n), 1)
    return jnp.broadcast_to(jnp.sum(jnp.where(here, row, 0.0), axis=1, keepdims=True), (n, 128))


def tile_kernel(
    dims, info, got, gain, regw, regb, noise, noise_edge, liftw, liftb, midg, midw, midb, out,
    taps, field, lon, lines, upper, sides, bands, keep, raw, prod, edges, cols, rows_out, stage, sems,
):
    cin, ch, ct, fr, fl = dims
    bands_n = got.shape[0]
    cw = got.shape[2]
    tile_row, tile_rows = info[0], info[1]
    top, bottom = tile_row == 0, tile_row == tile_rows - 1
    spare = (bands_n - ct) // 2
    steps = bands.shape[0]
    wide = fl // 128

    cols[0] = column(liftb[...])
    cols[1] = column(midg[...]) * 0.5
    cols[2] = column(midb[...])

    def real(i):
        row = tile_row * ct - spare + i
        return jnp.logical_and(row >= 0, row < ct * tile_rows)

    blocks = regw.shape[0]
    for k in range(blocks):
        first, last = 1 + k, bands_n - 1 - k
        half_gain = column(gain[k:k + 1, :])[:, :1] * 0.5
        bias = column(regb[k:k + 1, :])[:, :1]

        def fill(i, _, k=k, half_gain=half_gain):
            source = got[i] if k == 0 else field[i]
            values = activate(jnp.where(real(i), source.astype(F32), 0.0), half_gain)
            base = pl.multiple_of(i * 3 * cin, 16)
            taps[pl.ds(base, cin), :] = pltpu.roll(values, 1, 1).astype(BF16)
            taps[pl.ds(base + cin, cin), :] = values.astype(BF16)
            taps[pl.ds(base + 2 * cin, cin), :] = pltpu.roll(values, cw - 1, 1).astype(BF16)
            return 0

        lax.fori_loop(first, last, fill, 0, unroll=2)

        def conv(i, _, k=k, bias=bias):
            base = pl.multiple_of((i - 1) * 3 * cin, 16)
            update = jnp.dot(regw[k], taps[pl.ds(base, 9 * cin), :], preferred_element_type=F32)
            source = got[i] if k == 0 else field[i]
            field[i] = jnp.where(real(i), source.astype(F32) + update + bias, 0.0).astype(BF16)
            return 0

        lax.fori_loop(first + 1, last - 1, conv, 0, unroll=2)

    first = 1 + blocks
    count = bands_n - 2 * first

    def lon_split(fine_col):
        lower, part = split(2 * fine_col + 1 - LON_UP + 2 * LON_UP, LON_UP)
        return lower - 1, part

    position = lax.broadcasted_iota(jnp.int32, (1, 3 * fl), 1)
    shift = jnp.where(position >= 2 * fl, 2, jnp.where(position >= fl, 1, 0))
    lower, part = lon_split(position - shift * fl + shift - 1)
    low_lane = jnp.where(lower < 0, lower + cw, lower)
    high_lane = jnp.where(lower + 1 < 0, lower + 1 + cw, lower + 1)
    coarse_lane = lax.broadcasted_iota(jnp.int32, (cw, 3 * fl), 0)
    lon[...] = jnp.where(coarse_lane == low_lane, 1.0 - part,
                         jnp.where(coarse_lane == high_lane, part, 0.0)).astype(BF16)

    def widen(i, _):
        for q in range(3):
            lines[i, q * cin:(q + 1) * cin, :] = jnp.dot(
                field[i + first], lon[:, q * fl:(q + 1) * fl], preferred_element_type=F32)
        return 0

    lax.fori_loop(0, count, widen, 0, unroll=2)

    low_line = jnp.where(top, 1, 0)
    high_line = jnp.where(bottom, count - 2, count - 1)
    fine_total = fr * tile_rows

    def inside(t):
        row = tile_row * fr + t - 2
        return jnp.logical_and(row >= 0, row < fine_total)

    def lat_split(t):
        lower, part = split(2 * (t - 2) + 1 - LAT_UP + 2 * LAT_UP, LAT_UP)
        return jnp.clip(lower, low_line, high_line), jnp.clip(lower + 1, low_line, high_line), part

    nrows = noise.shape[1]
    slab = 3 * cin + nrows

    def raise_row(t, slot):
        a, b, part = lat_split(t)
        ok = inside(t)
        wa = jnp.where(ok, 1.0 - part, 0.0)
        wb = jnp.where(ok, part, 0.0)
        for o in range(0, 3 * cin, 16):
            upper[slot, o:o + 16, :] = (wa * lines[a, o:o + 16, :] + wb * lines[b, o:o + 16, :]).astype(BF16)
        upper[slot, 3 * cin:slab, :] = noise[t]

    lane = lax.broadcasted_iota(jnp.int32, (1, 128), 1)
    edge_row = jnp.where(lane < HALF, lane, lane - HALF)
    near = fl // LON_UP
    picked_cols = [-1, 0, near - 1, near]
    select_lane = lax.broadcasted_iota(jnp.int32, (cw, 128), 0)
    select_pos = lax.broadcasted_iota(jnp.int32, (cw, 128), 1)
    hits = jnp.zeros((cw, 128), jnp.bool_)
    for s, col in enumerate(picked_cols):
        hits = jnp.logical_or(hits, jnp.logical_and(select_pos == s, select_lane == col % cw))
    chosen = jnp.where(hits, 1.0, 0.0).astype(BF16)
    packed = jnp.zeros((cin, 128), F32)
    for i in range(count):
        narrow = jnp.dot(field[first + i], chosen, preferred_element_type=F32)
        packed = packed + (pltpu.roll(narrow, 4 * i, 1) if i else narrow)
    packed = packed.astype(BF16)
    key = lax.broadcasted_iota(jnp.int32, (128, 1), 0)
    key_line = key // 4
    key_pick = key - 4 * key_line
    key_col = jnp.where(key_pick == 0, picked_cols[0], jnp.where(
        key_pick == 1, picked_cols[1], jnp.where(key_pick == 2, picked_cols[2], picked_cols[3])))
    for p in range(3):
        t = edge_row + p
        a, b, part = lat_split(t)
        ok = inside(t)
        wa = jnp.where(ok, 1.0 - part, 0.0)
        wb = jnp.where(ok, part, 0.0)
        by_row = jnp.where(key_line == a, wa, 0.0) + jnp.where(key_line == b, wb, 0.0)
        for q in range(3):
            lower, part_m = lon_split(jnp.where(lane < HALF, q - 2, fl - 1 + q))
            by_col = jnp.where(key_col == lower, 1.0 - part_m, jnp.where(key_col == lower + 1, part_m, 0.0))
            base = p * slab + q * cin
            sides[base:base + cin, :] = jnp.dot(
                packed, (by_row * by_col).astype(BF16), preferred_element_type=F32).astype(BF16)
        sides[p * slab + 3 * cin:(p + 1) * slab, :] = noise_edge[p]
    edge_lift = jnp.dot(liftw[...], sides[...], preferred_element_type=F32) + cols[0]
    edge_lift = edge_lift.astype(BF16).astype(F32)
    edges[...] = jnp.where(inside(edge_row + 1), activate(edge_lift, cols[1]), 0.0)

    lane_first, lane_last = lane == 0, lane == 127

    def lift(slot):
        window = jnp.concatenate([upper[(slot + n) % steps] for n in range(3)], axis=0)
        raw[slot % 2] = jnp.dot(liftw[...], window, preferred_element_type=F32)

    def finish(l, slot):
        squares = jnp.zeros((8, fl), F32)
        for o in range(0, ch, 16):
            bias = jnp.concatenate([cols[0, o:o + 16, :]] * wide, axis=1)
            rounded = (raw[slot % 2, o:o + 16, :] + bias).astype(BF16)
            keep[slot, o:o + 16, :] = rounded
            values = rounded.astype(F32)
            values = values * values
            squares = squares + (values[:8] + values[8:])
        inverse = lax.rsqrt(jnp.sum(squares, axis=0, keepdims=True) * (1.0 / ch) + EPSILON)
        inverse = jnp.where(inside(l + 1), inverse, 0.0)
        for o in range(0, ch, 16):
            half_gain = jnp.concatenate([cols[1, o:o + 16, :]] * wide, axis=1)
            half = keep[slot, o:o + 16, :].astype(F32) * inverse * half_gain
            values = half + half * jnp.tanh(half)
            edge = edges[o:o + 16, :]
            parts = [values[:, j * 128:(j + 1) * 128] for j in range(wide)]
            east = [pltpu.roll(v, 1, 1) for v in parts]
            west = [pltpu.roll(v, 127, 1) for v in parts]
            edge_l = pltpu.roll(edge, 128 - l, 1)
            edge_r = pltpu.roll(edge, 128 + HALF - 1 - l, 1)
            bands[slot, ch + o:ch + o + 16, :] = values.astype(BF16)
            bands[slot, o:o + 16, :] = jnp.concatenate(
                [jnp.where(lane_first, east[j - 1] if j else edge_l, east[j]) for j in range(wide)],
                axis=1).astype(BF16)
            bands[slot, 2 * ch + o:2 * ch + o + 16, :] = jnp.concatenate(
                [jnp.where(lane_last, west[j + 1] if j < wide - 1 else edge_r, west[j]) for j in range(wide)],
                axis=1).astype(BF16)

    def mid(slot):
        window = jnp.concatenate([bands[(slot + n) % steps] for n in range(3)], axis=0)
        prod[slot % 2] = jnp.dot(midw[...], window, preferred_element_type=F32)

    group = stage.shape[2]

    def flush(part):
        slot = part % 2

        def copy(n):
            return pltpu.make_async_copy(
                stage.at[n % 2], out.at[0, :, pl.ds(pl.multiple_of(n * group, group), group), :], sems.at[n % 2])

        @pl.when(part >= 2)
        def _():
            copy(part - 2).wait()

        def shrink(o, _):
            for j in range(wide):
                block = rows_out[j, pl.ds(pl.multiple_of(o * 8 * group, 8 * group), 8 * group), :]
                stage[slot, pl.ds(o * 8, 8), :, j * 128:(j + 1) * 128] = block.reshape(8, group, 128).astype(BF16)
            return 0

        lax.fori_loop(0, ch // 8, shrink, 0)
        copy(part).start()

    def emit(y, slot):
        spot = y % group
        for o in range(0, ch, 16):
            bias = cols[2, o:o + 16, :]
            for j in range(wide):
                at = slice(j * 128, (j + 1) * 128)
                total = keep[(slot + 1) % steps, o:o + 16, at].astype(F32) + prod[slot % 2, o:o + 16, at] + bias
                rows_out[j, pl.ds(spot + o * group, 16, stride=group), :] = total

    for t in range(3):
        raise_row(jnp.int32(t), t % steps)
    for l in range(3):
        lift(l % steps)
        raise_row(jnp.int32(l + 3), (l + 3) % steps)
        finish(jnp.int32(l), l % steps)

    def trip(i, _):
        for j in range(steps):
            l = i * steps + j + 3
            slot = (j + 3) % steps
            lift(slot)
            mid(j)
            raise_row(jnp.minimum(l + 3, fr + 3), (j + 6) % steps)
            finish(l, slot)
            emit(l - 3, j)

        @pl.when((i + 1) % (group // steps) == 0)
        def _():
            flush(i // (group // steps))
        return 0

    lax.fori_loop(0, fr // steps, trip, 0)
    parts = fr // group
    for n in range(max(parts - 2, 0), parts):
        pltpu.make_async_copy(stage.at[n % 2], out.at[0, :, pl.ds(n * group, group), :], sems.at[n % 2]).wait()


def tile_program(info, got, gain, regw, regb, noise, noise_edge, liftw, liftb, midg, midw, midb, ct):
    cin, cw = got.shape[1], got.shape[2]
    ch = liftw.shape[0]
    fr, fl = noise.shape[0] - 4, noise.shape[2]
    count = ct + 2
    group = 16
    steps = 4
    vmem = pl.BlockSpec(memory_space=pltpu.VMEM)
    slab = 3 * cin + noise.shape[1]
    return pl.pallas_call(
        functools.partial(tile_kernel, (cin, ch, ct, fr, fl)),
        out_shape=jax.ShapeDtypeStruct((1, ch, fr, fl), BF16),
        in_specs=[pl.BlockSpec(memory_space=pltpu.SMEM)] + [vmem] * 11,
        out_specs=pl.BlockSpec(memory_space=pl.ANY),
        scratch_shapes=[
            pltpu.VMEM((got.shape[0] * 3 * cin, cw), BF16),
            pltpu.VMEM(got.shape, BF16),
            pltpu.VMEM((cw, 3 * fl), BF16),
            pltpu.VMEM((count, 3 * cin, fl), F32),
            pltpu.VMEM((steps, slab, fl), BF16),
            pltpu.VMEM((3 * slab, 128), BF16),
            pltpu.VMEM((steps, 3 * ch, fl), BF16),
            pltpu.VMEM((steps, ch, fl), BF16),
            pltpu.VMEM((2, ch, fl), F32),
            pltpu.VMEM((2, ch, fl), F32),
            pltpu.VMEM((ch, 128), F32),
            pltpu.VMEM((3, ch, 128), F32),
            pltpu.VMEM((fl // 128, ch * group, 128), F32),
            pltpu.VMEM((2, ch, group, fl), BF16),
            pltpu.SemaphoreType.DMA((2,)),
        ],
        compiler_params=pltpu.CompilerParams(vmem_limit_bytes=60_000_000),
    )(info, got, gain, regw, regb, noise, noise_edge, liftw, liftb, midg, midw, midb)


def per_device(
    coarse, reg_gain, reg_weight, reg_bias, noisy, lift_weight, lift_bias, mid_gain, mid_weight, mid_bias,
):
    device = lax.axis_index("lat")
    tile_rows = lax.axis_size("lat") // TILE_COLS
    cin, band_rows, clon = coarse.shape
    ct = band_rows * TILE_COLS
    ct_lon = clon // TILE_COLS
    blocks = reg_weight.shape[0]
    ch = lift_weight.shape[2]
    nout = noisy.shape[1]
    fr, fl = noisy.shape[2], noisy.shape[3]

    wide = coarse.reshape(cin, band_rows, TILE_COLS, ct_lon)
    after = jnp.roll(wide, -1, axis=2)
    before = jnp.roll(wide, 1, axis=2)
    side = jnp.where(jnp.arange(ct_lon) < ct_lon // 2, after, before)
    pieces = jnp.concatenate([wide, side], axis=3).transpose(2, 1, 0, 3)

    tile = noisy[0]
    edge_cols = jnp.concatenate([tile[:, :, :2], tile[:, :, -2:]], axis=2).transpose(0, 2, 1)
    edge_cols = jnp.pad(edge_cols.reshape(nout * 4, fr), ((0, 0), (0, 128 - fr)))
    edge_rows = jnp.concatenate([tile[:, :2], tile[:, -2:]], axis=1).reshape(nout * 4, fl)

    got, got_cols, got_rows = gather(pieces, edge_cols, edge_rows)

    tile_row = device // TILE_COLS
    has_north = tile_row > 0
    has_south = tile_row < tile_rows - 1
    nc = got_cols[:, :, :fr].reshape(6, nout, 4, fr).transpose(0, 1, 3, 2)
    nr = got_rows.reshape(2, nout, 4, fl)
    zero = jnp.zeros((), BF16)
    north = jnp.where(has_north, jnp.concatenate([nc[2][:, -2:, 2:], nr[0][:, 2:], nc[3][:, -2:, :2]], axis=2), zero)
    south = jnp.where(has_south, jnp.concatenate([nc[4][:, :2, 2:], nr[1][:, :2], nc[5][:, :2, :2]], axis=2), zero)
    middle = jnp.concatenate([nc[0][:, :, 2:], tile, nc[1][:, :, :2]], axis=2)
    whole = jnp.concatenate([north, middle, south], axis=1).transpose(1, 0, 2)
    spare = (-3 * nout) % 16
    noise = jnp.concatenate(
        [whole[:, :, 1 + q:1 + q + fl] for q in range(3)] + [jnp.zeros((fr + 4, spare, fl), BF16)], axis=1)
    sides = []
    for p in range(3):
        per_shift = []
        for q in range(3):
            lo = jnp.pad(whole[p:p + fr + 2, :, q].T, ((0, 0), (0, HALF - fr - 2)))
            hi = jnp.pad(whole[p:p + fr + 2, :, fl + 1 + q].T, ((0, 0), (0, HALF - fr - 2)))
            per_shift.append(jnp.concatenate([lo, hi], axis=1))
        sides.append(jnp.concatenate(per_shift + [jnp.zeros((spare, 128), BF16)], axis=0))
    noise_edge = jnp.stack(sides)

    regw = reg_weight.transpose(0, 3, 1, 2, 4).reshape(blocks, cin, 9 * cin)
    up = lift_weight[..., :cin].transpose(2, 0, 1, 3).reshape(ch, 3, 3 * cin)
    down = lift_weight[..., cin:].transpose(2, 0, 1, 3).reshape(ch, 3, 3 * nout)
    liftw = jnp.concatenate([up, down, jnp.zeros((ch, 3, spare), BF16)], axis=2).reshape(ch, -1)
    midw = mid_weight.transpose(2, 0, 1, 3).reshape(ch, 9 * ch)
    info = jnp.stack([tile_row, jnp.int32(tile_rows)]).astype(jnp.int32)
    got = got.reshape((got.shape[0] * band_rows,) + got.shape[2:])
    return tile_program(
        info, got, reg_gain, regw, reg_bias, noise, noise_edge,
        liftw, lift_bias[None], mid_gain[None], midw, mid_bias[None], ct)


def solution(mesh):
    placed = (
        P(None, ("grp", "lat"), None),
        P(),
        P(),
        P(),
        P(("grp", "lat"), None, None, None),
        P(),
        P(),
        P(),
        P(),
        P(),
    )
    return jax.shard_map(
        per_device,
        mesh=mesh,
        in_specs=placed,
        out_specs=P(("grp", "lat"), None, None, None),
        check_vma=False,
    )
```

```python
import functools

import jax
import jax.numpy as jnp
from jax import lax
from jax.experimental import pallas as pl
from jax.experimental.pallas import tpu as pltpu
from jax.sharding import PartitionSpec as P

TILE_COLS = 4
LAT_UP = 4
LON_UP = 4
EPSILON = 1e-06
F32 = jnp.float32
BF16 = jnp.bfloat16
MESH = pl.DeviceIdType.MESH
HALF = 64


def gather_kernel(
    pieces, cols, rows, regs, lifts, mids, got, got_cols, got_rows, regw, liftw, midw,
    send, recv, nsend, nrecv, local,
):
    me = lax.axis_index("lat")
    tile_rows = lax.axis_size("lat") // TILE_COLS
    r = me // TILE_COLS
    c = me % TILE_COLS
    north, south = r > 0, r < tile_rows - 1

    barrier = pltpu.get_barrier_semaphore()

    def greet(target):
        pl.semaphore_signal(barrier, inc=1, device_id={"lat": target}, device_id_type=MESH)

    for k in range(1, TILE_COLS):
        greet(r * TILE_COLS + (c + k) % TILE_COLS)

    @pl.when(north)
    def _():
        for k in range(TILE_COLS):
            greet((r - 1) * TILE_COLS + k)

    @pl.when(south)
    def _():
        for k in range(TILE_COLS):
            greet((r + 1) * TILE_COLS + k)

    peers = TILE_COLS - 1 + jnp.where(north, TILE_COLS, 0) + jnp.where(south, TILE_COLS, 0)
    pl.semaphore_wait(barrier, peers)

    def remote(src, dst, ssem, rsem, target):
        return pltpu.make_async_remote_copy(
            src_ref=src, dst_ref=dst, send_sem=ssem, recv_sem=rsem,
            device_id={"lat": target}, device_id_type=MESH)

    whole, upper, lower = pl.ds(0, 3), pl.ds(0, 2), pl.ds(1, 2)

    def band_copy(k, row, slot, ssem, part=whole):
        col = (c + k) % TILE_COLS
        return remote(pieces.at[col, part], got.at[slot, part], send.at[ssem], recv.at[slot], row * TILE_COLS + col)

    west, east = (c + TILE_COLS - 1) % TILE_COLS, (c + 1) % TILE_COLS

    def col_copy(slot, row, col):
        return remote(cols, got_cols.at[slot], nsend.at[slot], nrecv.at[slot], row * TILE_COLS + col)

    def row_copy(slot, row):
        return remote(rows, got_rows.at[slot], nsend.at[8 + slot], nrecv.at[8 + slot], row * TILE_COLS + c)

    def each(action):
        for col, side, row, slot, part in (
            (2, south, r + 1, 0, lower), (3, south, r + 1, 1, whole),
            (0, north, r - 1, 6, whole), (1, north, r - 1, 7, upper),
        ):
            @pl.when(jnp.logical_and(side, c == col))
            def _():
                for k in range(TILE_COLS):
                    action(band_copy(k, row, slot, TILE_COLS + k, part))

        for k in range(1, TILE_COLS):
            action(band_copy(k, r, 2 + c, k))
        action(col_copy(0, r, east))
        action(col_copy(1, r, west))

        @pl.when(south)
        def _():
            action(row_copy(0, r + 1))
            action(col_copy(6, r + 1, c))
            action(col_copy(2, r + 1, east))
            action(col_copy(3, r + 1, west))

        @pl.when(north)
        def _():
            action(row_copy(1, r - 1))
            action(col_copy(7, r - 1, c))
            action(col_copy(4, r - 1, east))
            action(col_copy(5, r - 1, west))

    each(lambda copy: copy.start())
    own = pltpu.make_async_copy(pieces.at[c], got.at[2 + c], local)
    own.start()

    cin, ch = regs.shape[2], mids.shape[1]
    nout = lifts.shape[2] - cin
    for k in range(regs.shape[0] // 9):
        for tap in range(9):
            regw[k, :, tap * cin:(tap + 1) * cin] = regs[9 * k + tap]
    for tap in range(9):
        midw[:, tap * ch:(tap + 1) * ch] = mids[tap]
    slab = liftw.shape[1] // 3
    for p in range(3):
        for q in range(3):
            base = p * slab + q * cin
            liftw[:, base:base + cin] = lifts[3 * p + q, :, :cin]
            base = p * slab + 3 * cin + q * nout
            liftw[:, base:base + nout] = lifts[3 * p + q, :, cin:]
        base = p * slab + 3 * (cin + nout)
        liftw[:, base:(p + 1) * slab] = jnp.zeros((ch, (p + 1) * slab - base), BF16)

    own.wait()
    each(lambda copy: copy.wait_send())

    def arrived(slot, part=whole):
        remote(pieces.at[0, part], got.at[slot, part], send.at[0], recv.at[slot], me).wait_recv()

    def edge(slot):
        if slot < 8:
            remote(cols, got_cols.at[slot], nsend.at[slot], nrecv.at[slot], me).wait_recv()
        else:
            remote(rows, got_rows.at[slot - 8], nsend.at[slot], nrecv.at[slot], me).wait_recv()

    for k in range(1, TILE_COLS):
        arrived(2 + (c + k) % TILE_COLS)
    edge(0)
    edge(1)

    @pl.when(north)
    def _():
        arrived(0, lower)
        arrived(1)
        for slot in (2, 3, 6, 8):
            edge(slot)

    @pl.when(south)
    def _():
        arrived(6)
        arrived(7, upper)
        for slot in (4, 5, 7, 9):
            edge(slot)


def gather(pieces, cols, rows, regs, lifts, mids, slab):
    any_space = pl.BlockSpec(memory_space=pl.ANY)
    vmem = pl.BlockSpec(memory_space=pltpu.VMEM)
    dma = pltpu.SemaphoreType.DMA
    cin, ch = regs.shape[2], mids.shape[1]
    return pl.pallas_call(
        gather_kernel,
        out_shape=(
            jax.ShapeDtypeStruct((8,) + pieces.shape[1:], BF16),
            jax.ShapeDtypeStruct((8,) + cols.shape, BF16),
            jax.ShapeDtypeStruct((2,) + rows.shape, BF16),
            jax.ShapeDtypeStruct((regs.shape[0] // 9, cin, 9 * cin), BF16),
            jax.ShapeDtypeStruct((ch, 3 * slab), BF16),
            jax.ShapeDtypeStruct((ch, 9 * ch), BF16),
        ),
        in_specs=[any_space] * 3 + [vmem] * 3,
        out_specs=(any_space,) * 3 + (vmem,) * 3,
        scratch_shapes=[dma((2 * TILE_COLS,)), dma((8,)), dma((10,)), dma((10,)), dma],
        compiler_params=pltpu.CompilerParams(collective_id=0, has_side_effects=True),
    )(pieces, cols, rows, regs, lifts, mids)


def activate(values, half_gain):
    inverse = lax.rsqrt(jnp.mean(values * values, axis=0, keepdims=True) + EPSILON)
    half = values * inverse * half_gain
    return half + half * jnp.tanh(half)


def split(numerator, factor):
    lower = numerator // (2 * factor)
    return lower, (numerator - 2 * factor * lower).astype(F32) / (2.0 * factor)


def column(row):
    n = row.shape[1]
    here = lax.broadcasted_iota(jnp.int32, (n, n), 0) == lax.broadcasted_iota(jnp.int32, (n, n), 1)
    return jnp.broadcast_to(jnp.sum(jnp.where(here, row, 0.0), axis=1, keepdims=True), (n, 128))


def tile_kernel(
    dims, got, gain, regw, regb, tile, own_cols, got_cols, got_rows, liftw, liftb, midg, midw, midb, out,
    grid, taps, field, lon, lines, upper, sides, bands, keep, raw, prod, edges, cols, rows_out, stage, sems,
):
    cin, ch, ct, fr, fl = dims
    bands_n, cw = field.shape[0], field.shape[2]
    tile_row, tile_rows = lax.axis_index("lat") // TILE_COLS, lax.axis_size("lat") // TILE_COLS
    nout = tile.shape[1]
    top, bottom = tile_row == 0, tile_row == tile_rows - 1
    spare = (bands_n - ct) // 2
    steps = bands.shape[0]
    wide = fl // 128

    cols[0] = column(liftb[...])
    cols[1] = column(midg[...]) * 0.5
    cols[2] = column(midb[...])

    def real(i):
        row = tile_row * ct - spare + i
        return jnp.logical_and(row >= 0, row < ct * tile_rows)

    blocks = regw.shape[0]
    for k in range(blocks):
        first, last = 1 + k, bands_n - 1 - k
        half_gain = column(gain[k:k + 1, :])[:, :1] * 0.5
        bias = column(regb[k:k + 1, :])[:, :1]

        def fill(i, values, half_gain=half_gain):
            values = activate(jnp.where(real(i), values, 0.0), half_gain)
            base = pl.multiple_of(i * 3 * cin, 16)
            taps[pl.ds(base, cin), :] = pltpu.roll(values, 1, 1).astype(BF16)
            taps[pl.ds(base + cin, cin), :] = values.astype(BF16)
            taps[pl.ds(base + 2 * cin, cin), :] = pltpu.roll(values, cw - 1, 1).astype(BF16)

        def fill_first(n, _, fill=fill):
            rims = got[n, 1].astype(F32)
            turned = pltpu.roll(rims, cw // 4, 1)
            for sub in range(2):
                rim = jnp.where(lax.broadcasted_iota(jnp.int32, (1, cw // 2), 1) < cw // 8,
                                turned if sub else rims, rims if sub else turned)
                values = jnp.concatenate([got[n, 2 * sub].astype(F32), rim], axis=1)
                field[2 * n + sub] = values.astype(BF16)
                fill(2 * n + sub, values)
            return 0

        def fill_next(i, _, fill=fill):
            fill(i, field[i].astype(F32))
            return 0

        if k == 0:
            lax.fori_loop(0, bands_n // 2, fill_first, 0)
        else:
            lax.fori_loop(first, last, fill_next, 0, unroll=2)

        def conv(i, _, k=k, bias=bias):
            base = pl.multiple_of((i - 1) * 3 * cin, 16)
            update = jnp.dot(regw[k], taps[pl.ds(base, 9 * cin), :], preferred_element_type=F32)
            field[i] = jnp.where(real(i), field[i].astype(F32) + update + bias, 0.0).astype(BF16)
            return 0

        lax.fori_loop(first + 1, last - 1, conv, 0, unroll=2)

    first = 1 + blocks
    count = bands_n - 2 * first

    def lon_split(fine_col):
        lower, part = split(2 * fine_col + 1 - LON_UP + 2 * LON_UP, LON_UP)
        return lower - 1, part

    position = lax.broadcasted_iota(jnp.int32, (1, 3 * fl), 1)
    shift = jnp.where(position >= 2 * fl, 2, jnp.where(position >= fl, 1, 0))
    lower, part = lon_split(position - shift * fl + shift - 1)
    low_lane = jnp.where(lower < 0, lower + cw, lower)
    high_lane = jnp.where(lower + 1 < 0, lower + 1 + cw, lower + 1)
    coarse_lane = lax.broadcasted_iota(jnp.int32, (cw, 3 * fl), 0)
    lon[...] = jnp.where(coarse_lane == low_lane, 1.0 - part,
                         jnp.where(coarse_lane == high_lane, part, 0.0)).astype(BF16)

    def widen(i, _):
        for q in range(3):
            lines[i, q * cin:(q + 1) * cin, :] = jnp.dot(
                field[i + first], lon[:, q * fl:(q + 1) * fl], preferred_element_type=F32)
        return 0

    lax.fori_loop(0, count, widen, 0, unroll=2)

    low_line = jnp.where(top, 1, 0)
    high_line = jnp.where(bottom, count - 2, count - 1)
    fine_total = fr * tile_rows

    def inside(t):
        row = tile_row * fr + t - 2
        return jnp.logical_and(row >= 0, row < fine_total)

    def lat_split(t):
        lower, part = split(2 * (t - 2) + 1 - LAT_UP + 2 * LAT_UP, LAT_UP)
        return jnp.clip(lower, low_line, high_line), jnp.clip(lower + 1, low_line, high_line), part

    slab = upper.shape[1]
    lane = lax.broadcasted_iota(jnp.int32, (1, 128), 1)
    lane_first, lane_last = lane == 0, lane == 127

    tall = fr + 4
    for n in range(nout):
        for j in range(wide):
            at = slice(j * 128, (j + 1) * 128)
            base = n * tall
            grid[j, base + 2:base + 2 + fr, :] = tile[0, n, :, at].astype(F32)
            above = got_rows[0, :, at].astype(F32)[4 * n + 2:4 * n + 4]
            below = got_rows[1, :, at].astype(F32)[4 * n:4 * n + 2]
            grid[j, base:base + 2, :] = jnp.where(top, 0.0, above)
            grid[j, base + 2 + fr:base + tall, :] = jnp.where(bottom, 0.0, below)

    def along(middle, above, below):
        above = jnp.where(top, 0.0, pltpu.roll(above.astype(F32), 128 - (fr - 2), 1))
        below = jnp.where(bottom, 0.0, pltpu.roll(below.astype(F32), fr + 2, 1))
        middle = pltpu.roll(middle.astype(F32), 2, 1)
        return jnp.where(lane < 2, above, jnp.where(lane < fr + 2, middle, below))

    west = along(got_cols[0], got_cols[2], got_cols[4])
    east = along(got_cols[1], got_cols[3], got_cols[5])
    here = along(own_cols[...], got_cols[6], got_cols[7])
    none = jnp.zeros((slab - 3 * (cin + nout), 128), F32)
    left_cols = jnp.concatenate([west[2 * nout:], here[:nout], none], axis=0)
    right_cols = jnp.concatenate([here[3 * nout:], east[:2 * nout], none], axis=0)
    west_col, east_col = west[3 * nout:], east[:nout]

    def noise_rows(t):
        rows = [grid[j, pl.ds(t, nout, stride=tall), :] for j in range(wide)]
        onward = [pltpu.roll(v, 1, 1) for v in rows]
        back = [pltpu.roll(v, 127, 1) for v in rows]
        edge_l = pltpu.roll(west_col, (128 - t) % 128 if isinstance(t, int) else 128 - t, 1)
        edge_r = pltpu.roll(east_col, 127 - t, 1)
        pieces = []
        for j in range(wide):
            lo = jnp.where(lane_first, onward[j - 1] if j else edge_l, onward[j])
            hi = jnp.where(lane_last, back[j + 1] if j < wide - 1 else edge_r, back[j])
            pieces.append(jnp.concatenate([lo, rows[j], hi, none], axis=0))
        return jnp.concatenate(pieces, axis=1).astype(BF16)

    def raise_row(t, slot):
        a, b, part = lat_split(jnp.int32(t))
        ok = inside(t)
        wa = jnp.where(ok, 1.0 - part, 0.0)
        wb = jnp.where(ok, part, 0.0)
        for o in range(0, 3 * cin, 16):
            upper[slot, o:o + 16, :] = (wa * lines[a, o:o + 16, :] + wb * lines[b, o:o + 16, :]).astype(BF16)
        upper[slot, 3 * cin:slab, :] = noise_rows(t)

    edge_row = jnp.where(lane < HALF, lane, lane - HALF)
    near = fl // LON_UP
    picked_cols = [-1, 0, near - 1, near]
    select_lane = lax.broadcasted_iota(jnp.int32, (cw, 128), 0)
    select_pos = lax.broadcasted_iota(jnp.int32, (cw, 128), 1)
    hits = jnp.zeros((cw, 128), jnp.bool_)
    for s, col in enumerate(picked_cols):
        hits = jnp.logical_or(hits, jnp.logical_and(select_pos == s, select_lane == col % cw))
    chosen = jnp.where(hits, 1.0, 0.0).astype(BF16)
    packed = jnp.zeros((cin, 128), F32)
    for i in range(count):
        narrow = jnp.dot(field[first + i], chosen, preferred_element_type=F32)
        packed = packed + (pltpu.roll(narrow, 4 * i, 1) if i else narrow)
    packed = packed.astype(BF16)
    key = lax.broadcasted_iota(jnp.int32, (128, 1), 0)
    key_line = key // 4
    key_pick = key - 4 * key_line
    key_col = jnp.where(key_pick == 0, picked_cols[0], jnp.where(
        key_pick == 1, picked_cols[1], jnp.where(key_pick == 2, picked_cols[2], picked_cols[3])))
    for p in range(3):
        t = edge_row + p
        a, b, part = lat_split(t)
        ok = inside(t)
        wa = jnp.where(ok, 1.0 - part, 0.0)
        wb = jnp.where(ok, part, 0.0)
        by_row = jnp.where(key_line == a, wa, 0.0) + jnp.where(key_line == b, wb, 0.0)
        for q in range(3):
            lower, part_m = lon_split(jnp.where(lane < HALF, q - 2, fl - 1 + q))
            by_col = jnp.where(key_col == lower, 1.0 - part_m, jnp.where(key_col == lower + 1, part_m, 0.0))
            base = p * slab + q * cin
            sides[base:base + cin, :] = jnp.dot(
                packed, (by_row * by_col).astype(BF16), preferred_element_type=F32).astype(BF16)
        sides[p * slab + 3 * cin:(p + 1) * slab, :] = jnp.where(
            lane < HALF, pltpu.roll(left_cols, (128 - p) % 128, 1), pltpu.roll(right_cols, HALF - p, 1)).astype(BF16)
    edge_lift = jnp.dot(liftw[...], sides[...], preferred_element_type=F32) + cols[0]
    edge_lift = edge_lift.astype(BF16).astype(F32)
    edges[...] = jnp.where(inside(edge_row + 1), activate(edge_lift, cols[1]), 0.0)

    def lift(slot):
        window = jnp.concatenate([upper[(slot + n) % steps] for n in range(3)], axis=0)
        raw[slot % 2] = jnp.dot(liftw[...], window, preferred_element_type=F32)

    def finish(l, slot):
        squares = jnp.zeros((8, fl), F32)
        for o in range(0, ch, 16):
            bias = jnp.concatenate([cols[0, o:o + 16, :]] * wide, axis=1)
            rounded = (raw[slot % 2, o:o + 16, :] + bias).astype(BF16)
            keep[slot, o:o + 16, :] = rounded
            values = rounded.astype(F32)
            values = values * values
            squares = squares + (values[:8] + values[8:])
        inverse = lax.rsqrt(jnp.sum(squares, axis=0, keepdims=True) * (1.0 / ch) + EPSILON)
        inverse = jnp.where(inside(l + 1), inverse, 0.0)
        for o in range(0, ch, 16):
            half_gain = jnp.concatenate([cols[1, o:o + 16, :]] * wide, axis=1)
            half = keep[slot, o:o + 16, :].astype(F32) * inverse * half_gain
            values = half + half * jnp.tanh(half)
            edge = edges[o:o + 16, :]
            parts = [values[:, j * 128:(j + 1) * 128] for j in range(wide)]
            east = [pltpu.roll(v, 1, 1) for v in parts]
            west = [pltpu.roll(v, 127, 1) for v in parts]
            edge_l = pltpu.roll(edge, 128 - l, 1)
            edge_r = pltpu.roll(edge, 128 + HALF - 1 - l, 1)
            bands[slot, ch + o:ch + o + 16, :] = values.astype(BF16)
            bands[slot, o:o + 16, :] = jnp.concatenate(
                [jnp.where(lane_first, east[j - 1] if j else edge_l, east[j]) for j in range(wide)],
                axis=1).astype(BF16)
            bands[slot, 2 * ch + o:2 * ch + o + 16, :] = jnp.concatenate(
                [jnp.where(lane_last, west[j + 1] if j < wide - 1 else edge_r, west[j]) for j in range(wide)],
                axis=1).astype(BF16)

    def mid(slot):
        window = jnp.concatenate([bands[(slot + n) % steps] for n in range(3)], axis=0)
        prod[slot % 2] = jnp.dot(midw[...], window, preferred_element_type=F32)

    group = stage.shape[2]

    def flush(part):
        slot = part % 2

        def copy(n):
            return pltpu.make_async_copy(
                stage.at[n % 2], out.at[0, :, pl.ds(pl.multiple_of(n * group, group), group), :], sems.at[n % 2])

        @pl.when(part >= 2)
        def _():
            copy(part - 2).wait()

        def shrink(o, _):
            for j in range(wide):
                block = rows_out[j, pl.ds(pl.multiple_of(o * 8 * group, 8 * group), 8 * group), :]
                stage[slot, pl.ds(o * 8, 8), :, j * 128:(j + 1) * 128] = block.reshape(8, group, 128).astype(BF16)
            return 0

        lax.fori_loop(0, ch // 8, shrink, 0)
        copy(part).start()

    def emit(y, slot):
        spot = y % group
        for o in range(0, ch, 16):
            bias = cols[2, o:o + 16, :]
            for j in range(wide):
                at = slice(j * 128, (j + 1) * 128)
                total = keep[(slot + 1) % steps, o:o + 16, at].astype(F32) + prod[slot % 2, o:o + 16, at] + bias
                rows_out[j, pl.ds(spot + o * group, 16, stride=group), :] = total

    for t in range(3):
        raise_row(t, t % steps)
    for l in range(3):
        lift(l % steps)
        raise_row(l + 3, (l + 3) % steps)
        finish(jnp.int32(l), l % steps)

    def trip(i, _):
        for j in range(steps):
            l = i * steps + j + 3
            slot = (j + 3) % steps
            lift(slot)
            mid(j)
            raise_row(jnp.minimum(l + 3, fr + 3), (j + 6) % steps)
            finish(l, slot)
            emit(l - 3, j)

        @pl.when((i + 1) % (group // steps) == 0)
        def _():
            flush(i // (group // steps))
        return 0

    lax.fori_loop(0, fr // steps, trip, 0)
    parts = fr // group
    for n in range(max(parts - 2, 0), parts):
        pltpu.make_async_copy(stage.at[n % 2], out.at[0, :, pl.ds(n * group, group), :], sems.at[n % 2]).wait()


def tile_program(got, gain, regw, regb, noisy, own_cols, got_cols, got_rows, liftw, liftb, midg, midw, midb, ct):
    cin, cw = got.shape[2], 2 * got.shape[3]
    ch = liftw.shape[0]
    nout, fr, fl = noisy.shape[1:]
    rows = 2 * got.shape[0]
    group = 16
    steps = 4
    vmem = pl.BlockSpec(memory_space=pltpu.VMEM)
    slab = liftw.shape[1] // 3
    return pl.pallas_call(
        functools.partial(tile_kernel, (cin, ch, ct, fr, fl)),
        out_shape=jax.ShapeDtypeStruct((1, ch, fr, fl), BF16),
        in_specs=[vmem] * 13,
        out_specs=pl.BlockSpec(memory_space=pl.ANY),
        scratch_shapes=[
            pltpu.VMEM((fl // 128, nout * (fr + 4), 128), F32),
            pltpu.VMEM((rows * 3 * cin, cw), BF16),
            pltpu.VMEM((rows, cin, cw), BF16),
            pltpu.VMEM((cw, 3 * fl), BF16),
            pltpu.VMEM((ct + 2, 3 * cin, fl), F32),
            pltpu.VMEM((steps, slab, fl), BF16),
            pltpu.VMEM((3 * slab, 128), BF16),
            pltpu.VMEM((steps, 3 * ch, fl), BF16),
            pltpu.VMEM((steps, ch, fl), BF16),
            pltpu.VMEM((2, ch, fl), F32),
            pltpu.VMEM((2, ch, fl), F32),
            pltpu.VMEM((ch, 128), F32),
            pltpu.VMEM((3, ch, 128), F32),
            pltpu.VMEM((fl // 128, ch * group, 128), F32),
            pltpu.VMEM((2, ch, group, fl), BF16),
            pltpu.SemaphoreType.DMA((2,)),
        ],
        compiler_params=pltpu.CompilerParams(vmem_limit_bytes=60_000_000),
    )(got, gain, regw, regb, noisy, own_cols, got_cols, got_rows, liftw, liftb, midg, midw, midb)


def per_device(
    coarse, reg_gain, reg_weight, reg_bias, noisy, lift_weight, lift_bias, mid_gain, mid_weight, mid_bias,
):
    cin, band_rows, clon = coarse.shape
    ct = band_rows * TILE_COLS
    ct_lon = clon // TILE_COLS
    blocks = reg_weight.shape[0]
    ch = lift_weight.shape[2]
    nout, fr, fl = noisy.shape[1:]

    quarter = ct_lon // 4
    centre = coarse.transpose(1, 0, 2).reshape(band_rows, cin, TILE_COLS, ct_lon)
    after = jnp.roll(centre[..., :quarter], -1, axis=2)
    before = jnp.roll(centre[..., -quarter:], 1, axis=2)
    rims = jnp.concatenate([after[0], before[0], after[1], before[1]], axis=-1)
    pieces = jnp.stack([centre[0], rims, centre[1]]).transpose(2, 0, 1, 3)

    tile = noisy[0]
    edge_cols = jnp.concatenate([tile[:, :, :2], tile[:, :, -2:]], axis=2).transpose(2, 0, 1)
    edge_cols = jnp.pad(edge_cols.reshape(4 * nout, fr), ((0, 0), (0, 128 - fr)))
    edge_rows = jnp.concatenate([tile[:, :2], tile[:, -2:]], axis=1).reshape(4 * nout, fl)

    slab = 3 * cin + -(-3 * nout // 16) * 16
    got, got_cols, got_rows, regw, liftw, midw = gather(
        pieces, edge_cols, edge_rows, reg_weight.reshape((9 * blocks,) + reg_weight.shape[3:]),
        lift_weight.reshape((9,) + lift_weight.shape[2:]), mid_weight.reshape((9,) + mid_weight.shape[2:]), slab)
    return tile_program(
        got, reg_gain, regw, reg_bias, noisy, edge_cols, got_cols, got_rows,
        liftw, lift_bias[None], mid_gain[None], midw, mid_bias[None], ct)


def solution(mesh):
    placed = (
        P(None, ("grp", "lat"), None),
        P(),
        P(),
        P(),
        P(("grp", "lat"), None, None, None),
        P(),
        P(),
        P(),
        P(),
        P(),
    )
    return jax.shard_map(
        per_device,
        mesh=mesh,
        in_specs=placed,
        out_specs=P(("grp", "lat"), None, None, None),
        check_vma=False,
    )
```

```python
import functools

import jax
import jax.numpy as jnp
from jax import lax
from jax.experimental import pallas as pl
from jax.experimental.pallas import tpu as pltpu
from jax.sharding import PartitionSpec as P

TILE_COLS = 4
LAT_UP = 4
LON_UP = 4
EPSILON = 1e-06
F32 = jnp.float32
BF16 = jnp.bfloat16
MESH = pl.DeviceIdType.MESH
HALF = 64


def gather_kernel(
    pieces, cols, rows, regs, lifts, mids, got, got_cols, got_rows, regw, liftw, midw,
    send, recv, nsend, nrecv, local,
):
    me = lax.axis_index("lat")
    tile_rows = lax.axis_size("lat") // TILE_COLS
    r = me // TILE_COLS
    c = me % TILE_COLS
    north, south = r > 0, r < tile_rows - 1

    barrier = pltpu.get_barrier_semaphore()

    def greet(target):
        pl.semaphore_signal(barrier, inc=1, device_id={"lat": target}, device_id_type=MESH)

    for k in range(1, TILE_COLS):
        greet(r * TILE_COLS + (c + k) % TILE_COLS)

    @pl.when(north)
    def _():
        for k in range(TILE_COLS):
            greet((r - 1) * TILE_COLS + k)

    @pl.when(south)
    def _():
        for k in range(TILE_COLS):
            greet((r + 1) * TILE_COLS + k)

    peers = TILE_COLS - 1 + jnp.where(north, TILE_COLS, 0) + jnp.where(south, TILE_COLS, 0)
    pl.semaphore_wait(barrier, peers)

    def remote(src, dst, ssem, rsem, target):
        return pltpu.make_async_remote_copy(
            src_ref=src, dst_ref=dst, send_sem=ssem, recv_sem=rsem,
            device_id={"lat": target}, device_id_type=MESH)

    whole, upper, lower = pl.ds(0, 2), pl.ds(0, 1), pl.ds(1, 1)

    def band_copy(k, row, slot, ssem, part=whole):
        col = (c + k) % TILE_COLS
        return remote(pieces.at[col, part], got.at[slot, part], send.at[ssem], recv.at[slot], row * TILE_COLS + col)

    west, east = (c + TILE_COLS - 1) % TILE_COLS, (c + 1) % TILE_COLS

    def col_copy(slot, row, col):
        return remote(cols, got_cols.at[slot], nsend.at[slot], nrecv.at[slot], row * TILE_COLS + col)

    def row_copy(slot, row):
        return remote(rows, got_rows.at[slot], nsend.at[8 + slot], nrecv.at[8 + slot], row * TILE_COLS + c)

    def each(action):
        for col, side, row, slot, part in (
            (2, south, r + 1, 0, lower), (3, south, r + 1, 1, whole),
            (0, north, r - 1, 6, whole), (1, north, r - 1, 7, upper),
        ):
            @pl.when(jnp.logical_and(side, c == col))
            def _():
                for k in range(TILE_COLS):
                    action(band_copy(k, row, slot, TILE_COLS + k, part))

        for k in range(1, TILE_COLS):
            action(band_copy(k, r, 2 + c, k))
        action(col_copy(0, r, east))
        action(col_copy(1, r, west))

        @pl.when(south)
        def _():
            action(row_copy(0, r + 1))
            action(col_copy(6, r + 1, c))
            action(col_copy(2, r + 1, east))
            action(col_copy(3, r + 1, west))

        @pl.when(north)
        def _():
            action(row_copy(1, r - 1))
            action(col_copy(7, r - 1, c))
            action(col_copy(4, r - 1, east))
            action(col_copy(5, r - 1, west))

    each(lambda copy: copy.start())
    own = pltpu.make_async_copy(pieces.at[c], got.at[2 + c], local)
    own.start()

    cin, ch = regs.shape[2], mids.shape[1]
    nout = lifts.shape[2] - cin
    for k in range(regs.shape[0] // 9):
        for tap in range(9):
            regw[k, :, tap * cin:(tap + 1) * cin] = regs[9 * k + tap]
    for tap in range(9):
        midw[:, tap * ch:(tap + 1) * ch] = mids[tap]
    slab = liftw.shape[1] // 3
    for p in range(3):
        for q in range(3):
            base = p * slab + q * cin
            liftw[:, base:base + cin] = lifts[3 * p + q, :, :cin]
            base = p * slab + 3 * cin + q * nout
            liftw[:, base:base + nout] = lifts[3 * p + q, :, cin:]
        base = p * slab + 3 * (cin + nout)
        liftw[:, base:(p + 1) * slab] = jnp.zeros((ch, (p + 1) * slab - base), BF16)

    own.wait()
    each(lambda copy: copy.wait_send())

    def arrived(slot, part=whole):
        remote(pieces.at[0, part], got.at[slot, part], send.at[0], recv.at[slot], me).wait_recv()

    def edge(slot):
        if slot < 8:
            remote(cols, got_cols.at[slot], nsend.at[slot], nrecv.at[slot], me).wait_recv()
        else:
            remote(rows, got_rows.at[slot - 8], nsend.at[slot], nrecv.at[slot], me).wait_recv()

    for k in range(1, TILE_COLS):
        arrived(2 + (c + k) % TILE_COLS)
    edge(0)
    edge(1)

    @pl.when(north)
    def _():
        arrived(0, lower)
        arrived(1)
        for slot in (2, 3, 6, 8):
            edge(slot)

    @pl.when(south)
    def _():
        arrived(6)
        arrived(7, upper)
        for slot in (4, 5, 7, 9):
            edge(slot)


def gather(pieces, cols, rows, regs, lifts, mids, slab):
    any_space = pl.BlockSpec(memory_space=pl.ANY)
    vmem = pl.BlockSpec(memory_space=pltpu.VMEM)
    dma = pltpu.SemaphoreType.DMA
    cin, ch = regs.shape[2], mids.shape[1]
    return pl.pallas_call(
        gather_kernel,
        out_shape=(
            jax.ShapeDtypeStruct((8,) + pieces.shape[1:], BF16),
            jax.ShapeDtypeStruct((8,) + cols.shape, BF16),
            jax.ShapeDtypeStruct((2,) + rows.shape, BF16),
            jax.ShapeDtypeStruct((regs.shape[0] // 9, cin, 9 * cin), BF16),
            jax.ShapeDtypeStruct((ch, 3 * slab), BF16),
            jax.ShapeDtypeStruct((ch, 9 * ch), BF16),
        ),
        in_specs=[any_space] * 3 + [vmem] * 3,
        out_specs=(any_space,) * 3 + (vmem,) * 3,
        scratch_shapes=[dma((2 * TILE_COLS,)), dma((8,)), dma((10,)), dma((10,)), dma],
        compiler_params=pltpu.CompilerParams(collective_id=0, has_side_effects=True),
    )(pieces, cols, rows, regs, lifts, mids)


def activate(values, half_gain):
    inverse = lax.rsqrt(jnp.mean(values * values, axis=0, keepdims=True) + EPSILON)
    half = values * inverse * half_gain
    return half + half * jnp.tanh(half)


def split(numerator, factor):
    lower = numerator // (2 * factor)
    return lower, (numerator - 2 * factor * lower).astype(F32) / (2.0 * factor)


def column(row):
    n = row.shape[1]
    here = lax.broadcasted_iota(jnp.int32, (n, n), 0) == lax.broadcasted_iota(jnp.int32, (n, n), 1)
    return jnp.broadcast_to(jnp.sum(jnp.where(here, row, 0.0), axis=1, keepdims=True), (n, 128))


def tile_kernel(
    dims, got, gain, regw, regb, tile, own_cols, got_cols, got_rows, liftw, liftb, midg, midw, midb, out,
    grid, taps, field, lon, lines, upper, sides, bands, keep, raw, prod, edges, cols, rows_out, stage, sems,
):
    cin, ch, ct, fr, fl = dims
    bands_n, cw = field.shape[0], field.shape[2]
    tile_row, tile_rows = lax.axis_index("lat") // TILE_COLS, lax.axis_size("lat") // TILE_COLS
    nout = tile.shape[1]
    top, bottom = tile_row == 0, tile_row == tile_rows - 1
    spare = (bands_n - ct) // 2
    steps = bands.shape[0]
    wide = fl // 128

    cols[0] = column(liftb[...])
    cols[1] = column(midg[...]) * 0.5
    cols[2] = column(midb[...])

    def real(i):
        row = tile_row * ct - spare + i
        return jnp.logical_and(row >= 0, row < ct * tile_rows)

    blocks = regw.shape[0]
    for k in range(blocks):
        first, last = 1 + k, bands_n - 1 - k
        half_gain = column(gain[k:k + 1, :])[:, :1] * 0.5
        bias = column(regb[k:k + 1, :])[:, :1]

        def fill(i, values, half_gain=half_gain):
            values = activate(jnp.where(real(i), values, 0.0), half_gain)
            base = pl.multiple_of(i * 3 * cin, 16)
            taps[pl.ds(base, cin), :] = pltpu.roll(values, 1, 1).astype(BF16)
            taps[pl.ds(base + cin, cin), :] = values.astype(BF16)
            taps[pl.ds(base + 2 * cin, cin), :] = pltpu.roll(values, cw - 1, 1).astype(BF16)

        def fill_first(n, _, fill=fill):
            for sub in range(2):
                field[2 * n + sub] = got[n, sub]
                fill(2 * n + sub, got[n, sub].astype(F32))
            return 0

        def fill_next(i, _, fill=fill):
            fill(i, field[i].astype(F32))
            return 0

        if k == 0:
            lax.fori_loop(0, bands_n // 2, fill_first, 0)
        else:
            lax.fori_loop(first, last, fill_next, 0, unroll=2)

        def conv(i, _, k=k, bias=bias):
            base = pl.multiple_of((i - 1) * 3 * cin, 16)
            update = jnp.dot(regw[k], taps[pl.ds(base, 9 * cin), :], preferred_element_type=F32)
            field[i] = jnp.where(real(i), field[i].astype(F32) + update + bias, 0.0).astype(BF16)
            return 0

        lax.fori_loop(first + 1, last - 1, conv, 0, unroll=2)

    first = 1 + blocks
    count = bands_n - 2 * first

    def lon_split(fine_col):
        lower, part = split(2 * fine_col + 1 - LON_UP + 2 * LON_UP, LON_UP)
        return lower - 1, part

    position = lax.broadcasted_iota(jnp.int32, (1, 3 * fl), 1)
    shift = jnp.where(position >= 2 * fl, 2, jnp.where(position >= fl, 1, 0))
    lower, part = lon_split(position - shift * fl + shift - 1)
    low_lane = jnp.where(lower < 0, lower + cw, lower)
    high_lane = jnp.where(lower + 1 < 0, lower + 1 + cw, lower + 1)
    coarse_lane = lax.broadcasted_iota(jnp.int32, (cw, 3 * fl), 0)
    lon[...] = jnp.where(coarse_lane == low_lane, 1.0 - part,
                         jnp.where(coarse_lane == high_lane, part, 0.0)).astype(BF16)

    def widen(i, _):
        for q in range(3):
            lines[i, q * cin:(q + 1) * cin, :] = jnp.dot(
                field[i + first], lon[:, q * fl:(q + 1) * fl], preferred_element_type=F32)
        return 0

    lax.fori_loop(0, count, widen, 0, unroll=2)

    low_line = jnp.where(top, 1, 0)
    high_line = jnp.where(bottom, count - 2, count - 1)
    fine_total = fr * tile_rows

    def inside(t):
        row = tile_row * fr + t - 2
        return jnp.logical_and(row >= 0, row < fine_total)

    def lat_split(t):
        lower, part = split(2 * (t - 2) + 1 - LAT_UP + 2 * LAT_UP, LAT_UP)
        return jnp.clip(lower, low_line, high_line), jnp.clip(lower + 1, low_line, high_line), part

    slab = upper.shape[1]
    lane = lax.broadcasted_iota(jnp.int32, (1, 128), 1)
    lane_first, lane_last = lane == 0, lane == 127

    tall = fr + 4
    for n in range(nout):
        for j in range(wide):
            at = slice(j * 128, (j + 1) * 128)
            base = n * tall
            grid[j, base + 2:base + 2 + fr, :] = tile[0, n, :, at].astype(F32)
            above = got_rows[0, :, at].astype(F32)[4 * n + 2:4 * n + 4]
            below = got_rows[1, :, at].astype(F32)[4 * n:4 * n + 2]
            grid[j, base:base + 2, :] = jnp.where(top, 0.0, above)
            grid[j, base + 2 + fr:base + tall, :] = jnp.where(bottom, 0.0, below)

    def along(middle, above, below):
        above = jnp.where(top, 0.0, pltpu.roll(above.astype(F32), 128 - (fr - 2), 1))
        below = jnp.where(bottom, 0.0, pltpu.roll(below.astype(F32), fr + 2, 1))
        middle = pltpu.roll(middle.astype(F32), 2, 1)
        return jnp.where(lane < 2, above, jnp.where(lane < fr + 2, middle, below))

    west = along(got_cols[0], got_cols[2], got_cols[4])
    east = along(got_cols[1], got_cols[3], got_cols[5])
    here = along(own_cols[...], got_cols[6], got_cols[7])
    none = jnp.zeros((slab - 3 * (cin + nout), 128), F32)
    left_cols = jnp.concatenate([west[2 * nout:], here[:nout], none], axis=0)
    right_cols = jnp.concatenate([here[3 * nout:], east[:2 * nout], none], axis=0)
    west_col, east_col = west[3 * nout:], east[:nout]

    def noise_rows(t):
        rows = [grid[j, pl.ds(t, nout, stride=tall), :] for j in range(wide)]
        onward = [pltpu.roll(v, 1, 1) for v in rows]
        back = [pltpu.roll(v, 127, 1) for v in rows]
        edge_l = pltpu.roll(west_col, (128 - t) % 128 if isinstance(t, int) else 128 - t, 1)
        edge_r = pltpu.roll(east_col, 127 - t, 1)
        pieces = []
        for j in range(wide):
            lo = jnp.where(lane_first, onward[j - 1] if j else edge_l, onward[j])
            hi = jnp.where(lane_last, back[j + 1] if j < wide - 1 else edge_r, back[j])
            pieces.append(jnp.concatenate([lo, rows[j], hi, none], axis=0))
        return jnp.concatenate(pieces, axis=1).astype(BF16)

    def raise_row(t, slot):
        a, b, part = lat_split(jnp.int32(t))
        ok = inside(t)
        wa = jnp.where(ok, 1.0 - part, 0.0)
        wb = jnp.where(ok, part, 0.0)
        for o in range(0, 3 * cin, 16):
            upper[slot, o:o + 16, :] = (wa * lines[a, o:o + 16, :] + wb * lines[b, o:o + 16, :]).astype(BF16)
        upper[slot, 3 * cin:slab, :] = noise_rows(t)

    edge_row = jnp.where(lane < HALF, lane, lane - HALF)
    near = fl // LON_UP
    picked_cols = [-1, 0, near - 1, near]
    select_lane = lax.broadcasted_iota(jnp.int32, (cw, 128), 0)
    select_pos = lax.broadcasted_iota(jnp.int32, (cw, 128), 1)
    hits = jnp.zeros((cw, 128), jnp.bool_)
    for s, col in enumerate(picked_cols):
        hits = jnp.logical_or(hits, jnp.logical_and(select_pos == s, select_lane == col % cw))
    chosen = jnp.where(hits, 1.0, 0.0).astype(BF16)
    packed = jnp.zeros((cin, 128), F32)
    for i in range(count):
        narrow = jnp.dot(field[first + i], chosen, preferred_element_type=F32)
        packed = packed + (pltpu.roll(narrow, 4 * i, 1) if i else narrow)
    packed = packed.astype(BF16)
    key = lax.broadcasted_iota(jnp.int32, (128, 1), 0)
    key_line = key // 4
    key_pick = key - 4 * key_line
    key_col = jnp.where(key_pick == 0, picked_cols[0], jnp.where(
        key_pick == 1, picked_cols[1], jnp.where(key_pick == 2, picked_cols[2], picked_cols[3])))
    for p in range(3):
        t = edge_row + p
        a, b, part = lat_split(t)
        ok = inside(t)
        wa = jnp.where(ok, 1.0 - part, 0.0)
        wb = jnp.where(ok, part, 0.0)
        by_row = jnp.where(key_line == a, wa, 0.0) + jnp.where(key_line == b, wb, 0.0)
        for q in range(3):
            lower, part_m = lon_split(jnp.where(lane < HALF, q - 2, fl - 1 + q))
            by_col = jnp.where(key_col == lower, 1.0 - part_m, jnp.where(key_col == lower + 1, part_m, 0.0))
            base = p * slab + q * cin
            sides[base:base + cin, :] = jnp.dot(
                packed, (by_row * by_col).astype(BF16), preferred_element_type=F32).astype(BF16)
        sides[p * slab + 3 * cin:(p + 1) * slab, :] = jnp.where(
            lane < HALF, pltpu.roll(left_cols, (128 - p) % 128, 1), pltpu.roll(right_cols, HALF - p, 1)).astype(BF16)
    edge_lift = jnp.dot(liftw[...], sides[...], preferred_element_type=F32) + cols[0]
    edge_lift = edge_lift.astype(BF16).astype(F32)
    edges[...] = jnp.where(inside(edge_row + 1), activate(edge_lift, cols[1]), 0.0)

    def lift(slot):
        window = jnp.concatenate([upper[(slot + n) % steps] for n in range(3)], axis=0)
        raw[slot % 2] = jnp.dot(liftw[...], window, preferred_element_type=F32)

    def finish(l, slot):
        squares = jnp.zeros((8, fl), F32)
        for o in range(0, ch, 16):
            bias = jnp.concatenate([cols[0, o:o + 16, :]] * wide, axis=1)
            rounded = (raw[slot % 2, o:o + 16, :] + bias).astype(BF16)
            keep[slot, o:o + 16, :] = rounded
            values = rounded.astype(F32)
            values = values * values
            squares = squares + (values[:8] + values[8:])
        inverse = lax.rsqrt(jnp.sum(squares, axis=0, keepdims=True) * (1.0 / ch) + EPSILON)
        inverse = jnp.where(inside(l + 1), inverse, 0.0)
        for o in range(0, ch, 16):
            half_gain = jnp.concatenate([cols[1, o:o + 16, :]] * wide, axis=1)
            half = keep[slot, o:o + 16, :].astype(F32) * inverse * half_gain
            values = half + half * jnp.tanh(half)
            edge = edges[o:o + 16, :]
            parts = [values[:, j * 128:(j + 1) * 128] for j in range(wide)]
            east = [pltpu.roll(v, 1, 1) for v in parts]
            west = [pltpu.roll(v, 127, 1) for v in parts]
            edge_l = pltpu.roll(edge, 128 - l, 1)
            edge_r = pltpu.roll(edge, 128 + HALF - 1 - l, 1)
            bands[slot, ch + o:ch + o + 16, :] = values.astype(BF16)
            bands[slot, o:o + 16, :] = jnp.concatenate(
                [jnp.where(lane_first, east[j - 1] if j else edge_l, east[j]) for j in range(wide)],
                axis=1).astype(BF16)
            bands[slot, 2 * ch + o:2 * ch + o + 16, :] = jnp.concatenate(
                [jnp.where(lane_last, west[j + 1] if j < wide - 1 else edge_r, west[j]) for j in range(wide)],
                axis=1).astype(BF16)

    def mid(slot):
        window = jnp.concatenate([bands[(slot + n) % steps] for n in range(3)], axis=0)
        prod[slot % 2] = jnp.dot(midw[...], window, preferred_element_type=F32)

    group = stage.shape[2]

    def flush(part):
        slot = part % 2

        def copy(n):
            return pltpu.make_async_copy(
                stage.at[n % 2], out.at[0, :, pl.ds(pl.multiple_of(n * group, group), group), :], sems.at[n % 2])

        @pl.when(part >= 2)
        def _():
            copy(part - 2).wait()

        def shrink(o, _):
            for j in range(wide):
                block = rows_out[j, pl.ds(pl.multiple_of(o * 8 * group, 8 * group), 8 * group), :]
                stage[slot, pl.ds(o * 8, 8), :, j * 128:(j + 1) * 128] = block.reshape(8, group, 128).astype(BF16)
            return 0

        lax.fori_loop(0, ch // 8, shrink, 0)
        copy(part).start()

    def emit(y, slot):
        spot = y % group
        for o in range(0, ch, 16):
            bias = cols[2, o:o + 16, :]
            for j in range(wide):
                at = slice(j * 128, (j + 1) * 128)
                total = keep[(slot + 1) % steps, o:o + 16, at].astype(F32) + prod[slot % 2, o:o + 16, at] + bias
                rows_out[j, pl.ds(spot + o * group, 16, stride=group), :] = total

    for t in range(3):
        raise_row(t, t % steps)
    for l in range(3):
        lift(l % steps)
        raise_row(l + 3, (l + 3) % steps)
        finish(jnp.int32(l), l % steps)

    def trip(i, _):
        for j in range(steps):
            l = i * steps + j + 3
            slot = (j + 3) % steps
            lift(slot)
            mid(j)
            raise_row(jnp.minimum(l + 3, fr + 3), (j + 6) % steps)
            finish(l, slot)
            emit(l - 3, j)

        @pl.when((i + 1) % (group // steps) == 0)
        def _():
            flush(i // (group // steps))
        return 0

    lax.fori_loop(0, fr // steps, trip, 0)
    parts = fr // group
    for n in range(max(parts - 2, 0), parts):
        pltpu.make_async_copy(stage.at[n % 2], out.at[0, :, pl.ds(n * group, group), :], sems.at[n % 2]).wait()


def tile_program(got, gain, regw, regb, noisy, own_cols, got_cols, got_rows, liftw, liftb, midg, midw, midb, ct):
    cin, cw = got.shape[2:]
    ch = liftw.shape[0]
    nout, fr, fl = noisy.shape[1:]
    rows = 2 * got.shape[0]
    group = 16
    steps = 4
    vmem = pl.BlockSpec(memory_space=pltpu.VMEM)
    slab = liftw.shape[1] // 3
    return pl.pallas_call(
        functools.partial(tile_kernel, (cin, ch, ct, fr, fl)),
        out_shape=jax.ShapeDtypeStruct((1, ch, fr, fl), BF16),
        in_specs=[vmem] * 13,
        out_specs=pl.BlockSpec(memory_space=pl.ANY),
        scratch_shapes=[
            pltpu.VMEM((fl // 128, nout * (fr + 4), 128), F32),
            pltpu.VMEM((rows * 3 * cin, cw), BF16),
            pltpu.VMEM((rows, cin, cw), BF16),
            pltpu.VMEM((cw, 3 * fl), BF16),
            pltpu.VMEM((ct + 2, 3 * cin, fl), F32),
            pltpu.VMEM((steps, slab, fl), BF16),
            pltpu.VMEM((3 * slab, 128), BF16),
            pltpu.VMEM((steps, 3 * ch, fl), BF16),
            pltpu.VMEM((steps, ch, fl), BF16),
            pltpu.VMEM((2, ch, fl), F32),
            pltpu.VMEM((2, ch, fl), F32),
            pltpu.VMEM((ch, 128), F32),
            pltpu.VMEM((3, ch, 128), F32),
            pltpu.VMEM((fl // 128, ch * group, 128), F32),
            pltpu.VMEM((2, ch, group, fl), BF16),
            pltpu.SemaphoreType.DMA((2,)),
        ],
        compiler_params=pltpu.CompilerParams(vmem_limit_bytes=60_000_000),
    )(got, gain, regw, regb, noisy, own_cols, got_cols, got_rows, liftw, liftb, midg, midw, midb)


def per_device(
    coarse, reg_gain, reg_weight, reg_bias, noisy, lift_weight, lift_bias, mid_gain, mid_weight, mid_bias,
):
    cin, band_rows, clon = coarse.shape
    ct = band_rows * TILE_COLS
    ct_lon = clon // TILE_COLS
    blocks = reg_weight.shape[0]
    ch = lift_weight.shape[2]
    nout, fr, fl = noisy.shape[1:]

    blocked = coarse.reshape(cin, band_rows, TILE_COLS, ct_lon)
    after = jnp.roll(blocked, -1, axis=2)
    before = jnp.roll(blocked, 1, axis=2)
    side = jnp.where(jnp.arange(ct_lon) < ct_lon // 2, after, before)
    pieces = jnp.concatenate([blocked, side], axis=3).transpose(2, 1, 0, 3)

    tile = noisy[0]
    edge_cols = jnp.concatenate([tile[:, :, :2], tile[:, :, -2:]], axis=2).transpose(2, 0, 1)
    edge_cols = jnp.pad(edge_cols.reshape(4 * nout, fr), ((0, 0), (0, 128 - fr)))
    edge_rows = jnp.concatenate([tile[:, :2], tile[:, -2:]], axis=1).reshape(4 * nout, fl)

    slab = 3 * cin + -(-3 * nout // 16) * 16
    got, got_cols, got_rows, regw, liftw, midw = gather(
        pieces, edge_cols, edge_rows, reg_weight.reshape((9 * blocks,) + reg_weight.shape[3:]),
        lift_weight.reshape((9,) + lift_weight.shape[2:]), mid_weight.reshape((9,) + mid_weight.shape[2:]), slab)
    return tile_program(
        got, reg_gain, regw, reg_bias, noisy, edge_cols, got_cols, got_rows,
        liftw, lift_bias[None], mid_gain[None], midw, mid_bias[None], ct)


def solution(mesh):
    placed = (
        P(None, ("grp", "lat"), None),
        P(),
        P(),
        P(),
        P(("grp", "lat"), None, None, None),
        P(),
        P(),
        P(),
        P(),
        P(),
    )
    return jax.shard_map(
        per_device,
        mesh=mesh,
        in_specs=placed,
        out_specs=P(("grp", "lat"), None, None, None),
        check_vma=False,
    )
```
